32 devices in a mesh: ctx: 8 (over y, x, core), seq: 4 (over z).
Axes of the slice: x: 2, y: 2, z: 4, core: 2. Of those that a mesh axis runs over, the one named last changes fastest.
Arguments:
- tokens: bfloat16 [4, 1024, 2560], P('seq', 'ctx'), may hold values from -6 to 6
- cotangent: bfloat16 [4, 1024, 2560], P('seq', 'ctx'), may hold values from -6 to 6
- gain_attn: bfloat16 [2560], P(('ctx', 'seq')), may hold values from 0.25 to 1.75
- w_query: bfloat16 [2560, 2560], P(('ctx', 'seq')), may hold values from -0.125 to 0.125
- w_keyval: bfloat16 [2560, 512], P(('ctx', 'seq')), may hold values from -0.125 to 0.125
- w_out: bfloat16 [2560, 2560], P(('ctx', 'seq')), may hold values from -6 to 6
- b_out: bfloat16 [2560], P(('ctx', 'seq')), may hold values from -4 to 4
- gain_ffn: bfloat16 [2560], P(('ctx', 'seq')), may hold values from 0.25 to 1.75
- w_gateup: bfloat16 [2560, 15360], P(('ctx', 'seq')), may hold values from -0.125 to 0.125
- w_down: bfloat16 [7680, 2560], P(('ctx', 'seq')), may hold values from -0.125 to 0.125
Outputs:
- output: bfloat16 [4, 1024, 2560], P('seq', 'ctx')
- input_grad: float32 [4, 1024, 2560], P('seq', 'ctx')
- gain_attn_grad: float32 [2560], P(('ctx', 'seq'))
- w_query_grad: float32 [2560, 2560], P('seq', 'ctx')
- w_keyval_grad: float32 [2560, 512], P('seq', 'ctx')
- w_out_grad: float32 [2560, 2560], P('ctx', 'seq')
- b_out_grad: float32 [2560], P(('ctx', 'seq'))
- gain_ffn_grad: float32 [2560], P(('ctx', 'seq'))
- w_gateup_grad: float32 [2560, 15360], P('seq', 'ctx')
- w_down_grad: float32 [7680, 2560], P('ctx', 'seq')
The draws below stay inside these ranges and needn't reach their ends.
All inputs are finite; a program needn't handle non-finite values.
Results may differ from the reference program's by a relative error of at most 0.017.
Values may be sent and summed in bfloat16 or wider, within the bound.
No kernel may reach another device: no remote copies, remote signals or barrier semaphores. Data moves between devices by JAX's collectives and lax.ppermute only.
A program may use at most 640 MiB of HBM per device.

```python
import jax
import jax.numpy as jnp
from jax import lax

D = 2560
NH = 10
HD = 256
FF = 7680
WINDOW = 2048
HQ = 2560
LEN = 1024
SEQS = 4


def block_levels(rng, dims, shards, low, high):
    def one(axis_at, blocks):
        heights = jax.random.uniform(jax.random.fold_in(jax.random.fold_in(rng, 6), axis_at), (blocks,), jnp.float32, low / len(shards), high / len(shards))
        return jnp.repeat(jnp.exp(heights), dims[axis_at] // blocks).reshape((-1,) + (1,) * (len(dims) - axis_at - 1))

    loudness = one(*shards[0])
    for cut in shards[1:]:
        loudness = loudness * one(*cut)
    return loudness


def normal_values(key, extent, deviation, bound, split=(), kind=jnp.bfloat16):
    loudness = block_levels(key, extent, split, -0.22, 0.18) if split else 1.0
    drawn = jax.random.normal(key, extent, jnp.float32) * deviation * loudness
    return jnp.minimum(jnp.maximum(drawn, -bound), bound).astype(kind)


def setup_inputs(seed: int = 0) -> dict:
    arg_keys = jax.random.split(jax.random.key(seed), 11)
    tokens = normal_values(arg_keys[0], (SEQS, LEN, D), 1.0, 6.0, ((0, 4), (1, 8)))
    cotangent = normal_values(arg_keys[1], (SEQS, LEN, D), 1.0, 6.0, ((0, 4), (1, 8)))
    gain_attn = jnp.clip(1.0 + 0.15 * jax.random.normal(arg_keys[2], (D,), jnp.float32), 0.25, 1.75).astype(jnp.bfloat16)
    w_query = normal_values(arg_keys[3], (D, HQ), D ** -0.5, 0.125, ((0, 32),))
    w_keyval = normal_values(arg_keys[4], (D, 2 * HD), D ** -0.5, 0.125, ((0, 32),))
    w_out = normal_values(arg_keys[5], (HQ, D), (max(1, HQ // WINDOW)) ** -0.5, 6.0, ((0, 32),))
    b_out = normal_values(arg_keys[6], (D,), 1.0, 4.0, ((0, 32),))
    gain_ffn = jnp.clip(1.0 + 0.15 * jax.random.normal(arg_keys[7], (D,), jnp.float32), 0.25, 1.75).astype(jnp.bfloat16)
    w_gateup = normal_values(arg_keys[8], (D, 2 * FF), D ** -0.5, 0.125, ((0, 32),))
    w_down = normal_values(arg_keys[9], (FF, D), (FF // 4) ** -0.5, 0.125, ((0, 32),))
    return dict(tokens=tokens, cotangent=cotangent, gain_attn=gain_attn, w_query=w_query, w_keyval=w_keyval, w_out=w_out, b_out=b_out, gain_ffn=gain_ffn, w_gateup=w_gateup, w_down=w_down)


EPS = 1e-06
NEG = -1e+30

def widen(low):
    return lax.optimization_barrier(low).astype(jnp.float32)

def norm_forward(residual, gain_vec):
    scale = lax.rsqrt(lax.optimization_barrier(jnp.mean(residual * residual, axis=-1, keepdims=True)) + EPS)
    normed = residual * scale
    return (normed, scale, (normed * gain_vec.astype(jnp.float32)).astype(jnp.bfloat16))

def norm_backward(d_in, normed, scale, gain_vec):
    d_normed = d_in * gain_vec.astype(jnp.float32)
    d_gain = lax.optimization_barrier(jnp.sum(d_in * normed, axis=0))
    d_resid = scale * (d_normed - normed * lax.optimization_barrier(jnp.mean(d_normed * normed, axis=-1, keepdims=True)))
    return (d_resid, d_gain)

def gelu_parts(gate_pre):
    gelu_val, pullback = jax.vjp(lambda v: jax.nn.gelu(v, approximate=True), gate_pre)
    return (gelu_val, pullback(jnp.ones_like(gate_pre))[0])

def dot_last(left, right):
    return lax.dot_general(left, right, (((1,), (1,)), ((), ())), preferred_element_type=jnp.float32)

def dot_first(left, right):
    return lax.dot_general(left, right, (((0,), (0,)), ((), ())), preferred_element_type=jnp.float32)

def allowed_mask(query_pos, key_pos):
    spacing = query_pos[:, None] - key_pos[None, :]
    return (spacing >= 0) & (spacing < WINDOW) & (key_pos[None, :] >= 0)

def reference(tokens, cotangent, gain_attn, w_query, w_keyval, w_out, b_out, gain_ffn, w_gateup, w_down):
    length = tokens.shape[1]
    block = min(512, length)
    count = length // block
    q_scale = HD ** (-0.5)
    key_pos = jnp.arange(length, dtype=jnp.int32)
    starts = jnp.arange(count, dtype=jnp.int32) * block

    def one_sequence(carry, inputs):
        seq_tokens, seq_cot = inputs
        residual = seq_tokens.astype(jnp.float32)
        normed1, scale1, hidden1 = norm_forward(residual, gain_attn)
        query = (jnp.dot(hidden1, w_query, preferred_element_type=jnp.float32) * q_scale).astype(jnp.bfloat16)
        keyval = jnp.dot(hidden1, w_keyval, preferred_element_type=jnp.float32).astype(jnp.bfloat16)
        key_wide = widen(keyval[:, :HD])
        value_wide = widen(keyval[:, HD:])
        query_blocks = query.reshape(count, block, NH, HD)

        def block_scores(query_block, start):
            query_pos = start + jnp.arange(block, dtype=jnp.int32)
            allowed = allowed_mask(query_pos, key_pos)
            scores = jnp.einsum('qhd,kd->hqk', widen(query_block), key_wide)
            return jnp.where(allowed[None], scores, NEG)

        def forward_block(inputs):
            query_block, start = inputs
            scores = block_scores(query_block, start)
            maximum = lax.optimization_barrier(jnp.max(scores, axis=-1, keepdims=True))
            log_total = maximum + jnp.log(lax.optimization_barrier(jnp.sum(jnp.exp(scores - maximum), axis=-1, keepdims=True)))
            probs_low = jnp.exp(scores - log_total).astype(jnp.bfloat16)
            mixed = jnp.einsum('hqk,kd->qhd', widen(probs_low), value_wide).astype(jnp.bfloat16)
            return (mixed, log_total)
        mixed_blocks, log_totals = lax.map(forward_block, (query_blocks, starts))
        mixed_flat = mixed_blocks.reshape(length, NH * HD)
        middle = residual + jnp.dot(mixed_flat, w_out, preferred_element_type=jnp.float32) + b_out.astype(jnp.float32)
        normed2, scale2, hidden2 = norm_forward(middle, gain_ffn)
        gateup = jnp.dot(hidden2, w_gateup, preferred_element_type=jnp.float32)
        gate_pre = gateup[:, :FF]
        up_pre = gateup[:, FF:]
        gelu_val, gelu_slope = gelu_parts(gate_pre)
        inner = (gelu_val * up_pre).astype(jnp.bfloat16)
        output = (middle + jnp.dot(inner, w_down, preferred_element_type=jnp.float32)).astype(jnp.bfloat16)
        d_inner = dot_last(seq_cot, w_down)
        down_grad = dot_first(inner, seq_cot)
        d_gateup = jnp.concatenate([d_inner * up_pre * gelu_slope, d_inner * gelu_val], axis=1).astype(jnp.bfloat16)
        gateup_grad = dot_first(hidden2, d_gateup)
        d_hidden2 = dot_last(d_gateup, w_gateup)
        d_middle_norm, d_gain2 = norm_backward(d_hidden2, normed2, scale2, gain_ffn)
        d_middle = seq_cot.astype(jnp.float32) + d_middle_norm
        d_bias = lax.optimization_barrier(jnp.sum(d_middle, axis=0))
        d_low = d_middle.astype(jnp.bfloat16)
        out_grad = dot_first(mixed_flat, d_low)
        d_mixed = dot_last(d_low, w_out).astype(jnp.bfloat16).reshape(count, block, NH, HD)

        def backward_block(accum, inputs):
            query_block, start, log_total, d_block = inputs
            scores = block_scores(query_block, start)
            probs = jnp.exp(scores - log_total)
            probs_low = probs.astype(jnp.bfloat16)
            d_wide = widen(d_block)
            d_probs = jnp.einsum('qhd,kd->hqk', d_wide, value_wide)
            delta = lax.optimization_barrier(jnp.sum(probs * d_probs, axis=-1, keepdims=True))
            d_scores = widen((probs * (d_probs - delta)).astype(jnp.bfloat16))
            d_query = (jnp.einsum('hqk,kd->qhd', d_scores, key_wide) * q_scale).astype(jnp.bfloat16)
            d_keys = jnp.einsum('hqk,qhd->kd', d_scores, widen(query_block))
            d_values = jnp.einsum('hqk,qhd->kd', widen(probs_low), d_wide)
            return (accum + jnp.concatenate([d_keys, d_values], axis=1), d_query)
        d_window, d_query_blocks = lax.scan(backward_block, jnp.zeros((length, 2 * HD), jnp.float32), (query_blocks, starts, log_totals, d_mixed))
        d_query_low = d_query_blocks.reshape(length, NH * HD)
        d_keyval_low = d_window.astype(jnp.bfloat16)
        query_grad = dot_first(hidden1, d_query_low)
        keyval_grad = dot_first(hidden1, d_keyval_low)
        d_hidden1 = dot_last(d_query_low, w_query) + dot_last(d_keyval_low, w_keyval)
        d_input_norm, d_gain1 = norm_backward(d_hidden1, normed1, scale1, gain_attn)
        d_input = d_middle + d_input_norm
        terms = (d_gain1, query_grad, keyval_grad, out_grad, d_bias, d_gain2, gateup_grad, down_grad)
        carry = tuple((total + term for total, term in zip(carry, terms)))
        return (carry, (output, d_input))
    zeros_all = (jnp.zeros((D,), jnp.float32), jnp.zeros((D, NH * HD), jnp.float32), jnp.zeros((D, 2 * HD), jnp.float32), jnp.zeros((NH * HD, D), jnp.float32), jnp.zeros((D,), jnp.float32), jnp.zeros((D,), jnp.float32), jnp.zeros((D, 2 * FF), jnp.float32), jnp.zeros((FF, D), jnp.float32))
    totals, (output, input_grad) = lax.scan(one_sequence, zeros_all, (tokens, cotangent))
    return (output, input_grad, totals[0], totals[1], totals[2], totals[3], totals[4], totals[5], totals[6], totals[7])
```

```python
import math

import jax
import jax.numpy as jnp
from jax import lax
from jax.sharding import Mesh, PartitionSpec as P

NH = 10
HD = 256
FF = 7680
WINDOW = 2048

EPS = 1e-06
NEG = -1e30

F32 = jnp.float32
BF16 = jnp.bfloat16

CHIP = ("hi", "lo")
CTX = ("hi", "lo", "core")
GROUP = ("hi", "lo", "core", "far")
SEQ = ("far", "near")
EVERY = ("hi", "lo", "core", "far", "near")


def dot(left, right):
    return jnp.dot(left, right, preferred_element_type=F32)


def dot_last(left, right):
    return lax.dot_general(left, right, (((1,), (1,)), ((), ())), preferred_element_type=F32)


def dot_first(left, right):
    return lax.dot_general(left, right, (((0,), (0,)), ((), ())), preferred_element_type=F32)


def swap(value, axis):
    count = lax.axis_size(axis)
    return lax.ppermute(value, axis, [(i, (i + 1) % count) for i in range(count)])


def chip_shifts():
    side_h, side_l = lax.axis_size("hi"), lax.axis_size("lo")
    return [(dh, dl) for dh in range(side_h) for dl in range(side_l)]


def to_chip(value, dh, dl):
    side_h, side_l = lax.axis_size("hi"), lax.axis_size("lo")
    if dh == 0 and dl == 0:
        return value
    pairs = []
    for h in range(side_h):
        for l in range(side_l):
            pairs.append((h * side_l + l, (h + dh) % side_h * side_l + (l + dl) % side_l))
    return lax.ppermute(value, CHIP, pairs)


def chip_from(dh, dl):
    side_h, side_l = lax.axis_size("hi"), lax.axis_size("lo")
    h, l = lax.axis_index("hi"), lax.axis_index("lo")
    return (h - dh) % side_h * side_l + (l - dl) % side_l


def chip_to(dh, dl):
    side_h, side_l = lax.axis_size("hi"), lax.axis_size("lo")
    h, l = lax.axis_index("hi"), lax.axis_index("lo")
    return (h + dh) % side_h * side_l + (l + dl) % side_l


def gather_ctx(block):
    core = lax.axis_index("core")
    shifts = chip_shifts()
    out = jnp.zeros((len(shifts), 2) + block.shape, block.dtype)
    for dh, dl in shifts:
        came = to_chip(block, dh, dl)
        chip = chip_from(dh, dl)
        out = lax.dynamic_update_slice(out, came[None, None], (chip, core, 0, 0))
        other = swap(came, "core")
        out = lax.dynamic_update_slice(out, other[None, None], (chip, 1 - core, 0, 0))
    return out.reshape((2 * len(shifts),) + block.shape)


def scatter_ctx(parts):
    core = lax.axis_index("core")
    shifts = chip_shifts()
    parts = parts.reshape((len(shifts), 2) + parts.shape[1:])
    mine = lax.dynamic_index_in_dim(parts, core, 1, False)
    theirs = lax.dynamic_index_in_dim(parts, 1 - core, 1, False)
    pair = mine.astype(F32) + swap(theirs, "core").astype(F32)
    low = pair.astype(BF16)
    total = lax.dynamic_index_in_dim(pair, chip_to(0, 0), 0, False)
    for dh, dl in shifts[1:]:
        piece = lax.dynamic_index_in_dim(low, chip_to(dh, dl), 0, False)
        total = total + to_chip(piece, dh, dl).astype(F32)
    return total


def exchange(value, axes):
    return lax.all_to_all(value, axes, split_axis=0, concat_axis=0, tiled=True)


def norm_scale(value):
    return lax.rsqrt(jnp.mean(value * value, axis=-1, keepdims=True) + EPS)


def norm_backward(d_in, normed, scale, gain_vec):
    d_normed = d_in * gain_vec.astype(F32)
    d_gain = jnp.sum(d_in * normed, axis=0)
    d_resid = scale * (d_normed - normed * jnp.mean(d_normed * normed, axis=-1, keepdims=True))
    return (d_resid, d_gain)


def gelu_parts(gate_pre):
    gelu_val, pullback = jax.vjp(lambda v: jax.nn.gelu(v, approximate=True), gate_pre)
    return (gelu_val, pullback(jnp.ones_like(gate_pre))[0])


def per_device(
    tokens, cotangent, gain_attn, w_query, w_keyval, w_out, b_out, gain_ffn, w_gateup, w_down
):
    block_len, width = tokens.shape[1:]
    n_ctx = lax.axis_size("hi") * lax.axis_size("lo") * lax.axis_size("core")
    n_far, n_near = lax.axis_size("far"), lax.axis_size("near")
    n_seq = n_far * n_near
    n_all = n_ctx * n_seq
    n_group = n_ctx * n_far
    rows = w_query.shape[0]
    length = n_ctx * block_len
    q_scale = HD ** (-0.5)
    position = (lax.axis_index("hi") * lax.axis_size("lo") + lax.axis_index("lo")) * 2 + lax.axis_index("core")
    far, near = lax.axis_index("far"), lax.axis_index("near")
    q_cols = NH * HD // n_ctx
    kv_cols = 2 * HD // n_ctx
    share = FF // n_group

    block = tokens.reshape(block_len, width)
    d_final = cotangent.reshape(block_len, width)

    vectors = jnp.stack([gain_attn, b_out, gain_ffn])
    vectors = exchange(jnp.broadcast_to(vectors[None], (n_all, 3, rows)), EVERY)
    vectors = vectors.transpose(1, 0, 2).reshape(3, width)
    gain1, bias, gain2 = vectors[0], vectors[1], vectors[2]
    qkv_send = jnp.concatenate(
        [w_query.reshape(rows, n_ctx, q_cols), w_keyval.reshape(rows, n_ctx, kv_cols)], axis=2
    ).transpose(1, 0, 2)
    qkv_send = jnp.broadcast_to(qkv_send[:, None], (n_ctx, n_seq) + qkv_send.shape[1:])
    w_qkv = exchange(qkv_send.reshape((n_all,) + qkv_send.shape[2:]), EVERY)
    w_qkv = w_qkv.reshape(width, q_cols + kv_cols)
    full_tokens = gather_ctx(block).reshape(length, width).astype(F32)
    full_out = lax.all_gather(w_out, EVERY, axis=0, tiled=True)

    gateup_send = w_gateup.reshape(rows, 2, n_group, share).transpose(2, 0, 1, 3)
    own_half = exchange(gateup_send.reshape(n_group, rows, 2 * share), GROUP)
    other_half = swap(own_half, "near")
    w_gu = jnp.zeros((n_group, n_near, rows, 2 * share), BF16)
    w_gu = lax.dynamic_update_slice(w_gu, own_half[:, None], (0, near, 0, 0))
    w_gu = lax.dynamic_update_slice(w_gu, other_half[:, None], (0, 1 - near, 0, 0))
    w_gu = w_gu.reshape(width, 2 * share)
    w_dn = jnp.zeros((n_near,) + w_down.shape, BF16)
    w_dn = lax.dynamic_update_slice(w_dn, w_down[None], (near, 0, 0))
    w_dn = lax.dynamic_update_slice(w_dn, swap(w_down, "near")[None], (1 - near, 0, 0))
    w_dn = w_dn.reshape(share, width)

    full_scale = norm_scale(full_tokens)
    hidden1 = (full_tokens * full_scale * gain1.astype(F32)).astype(BF16)
    qkv = dot(hidden1, w_qkv)
    q_part = (qkv[:, :q_cols] * q_scale).astype(BF16)
    kv_part = qkv[:, q_cols:].astype(BF16)
    query = exchange(q_part.reshape(n_ctx, block_len, q_cols), CTX)
    query = query.transpose(1, 0, 2).reshape(block_len, NH, HD)
    keyval = exchange(jnp.broadcast_to(kv_part[None], (n_ctx, length, kv_cols)), CTX)
    keyval = keyval.transpose(1, 0, 2).reshape(length, 2 * HD)
    key, value = keyval[:, :HD], keyval[:, HD:]
    spacing = (position * block_len + jnp.arange(block_len, dtype=jnp.int32))[:, None] - jnp.arange(
        length, dtype=jnp.int32
    )[None, :]
    allowed = (spacing >= 0) & (spacing < WINDOW)
    scores = jnp.einsum("qhd,kd->hqk", query, key, preferred_element_type=F32)
    scores = jnp.where(allowed[None], scores, NEG)
    maximum = jnp.max(scores, axis=-1, keepdims=True)
    log_total = maximum + jnp.log(jnp.sum(jnp.exp(scores - maximum), axis=-1, keepdims=True))
    probs_low = jnp.exp(scores - log_total).astype(BF16)
    mixed = jnp.einsum("hqk,kd->qhd", probs_low, value, preferred_element_type=F32).astype(BF16)
    mixed = mixed.reshape(block_len, NH * HD)
    residual = block.astype(F32)
    middle = residual + dot(mixed, full_out) + bias.astype(F32)

    scale2 = norm_scale(middle)
    normed2 = middle * scale2
    hidden2 = (normed2 * gain2.astype(F32)).astype(BF16)

    def gather_group(mine):
        theirs = swap(mine, "far")
        return [gather_ctx(v).reshape(length, width) for v in (mine, theirs)]

    def scatter_group(pieces):
        mine, theirs = [
            scatter_ctx(p.astype(BF16).reshape(n_ctx, block_len, width)) for p in pieces
        ]
        return mine + swap(theirs.astype(BF16), "far").astype(F32)

    final_rows = gather_group(d_final)
    hidden_rows = gather_group(hidden2)
    outs, backs, inners, d_gus = [], [], [], []
    for hidden, final in zip(hidden_rows, final_rows):
        gateup = dot(hidden, w_gu)
        gate_pre, up_pre = gateup[:, :share], gateup[:, share:]
        gelu_val, gelu_slope = gelu_parts(gate_pre)
        inner = (gelu_val * up_pre).astype(BF16)
        d_inner = dot_last(final, w_dn)
        d_gu = jnp.concatenate(
            [d_inner * up_pre * gelu_slope, d_inner * gelu_val], axis=1
        ).astype(BF16)
        outs.append(dot(inner, w_dn))
        backs.append(dot_last(d_gu, w_gu))
        inners.append(inner)
        d_gus.append(d_gu)
    d_hidden2 = scatter_group(backs)
    output = (middle + scatter_group(outs)).astype(BF16)

    inner_rows, d_gu_rows = jnp.concatenate(inners), jnp.concatenate(d_gus)
    hidden_all, final_all = jnp.concatenate(hidden_rows), jnp.concatenate(final_rows)
    gu_grad = dot_first(hidden_all, d_gu_rows).astype(BF16)
    down_grad = dot_first(inner_rows, final_all).astype(BF16)
    quarter = width // n_seq
    gu_grad = gu_grad.reshape(n_far, n_near, quarter, 2 * share)
    theirs = lax.dynamic_index_in_dim(gu_grad, 1 - near, 1, False)
    mine = lax.dynamic_index_in_dim(gu_grad, near, 1, False)
    gu_sum = (mine.astype(F32) + swap(theirs, "near").astype(F32)).astype(BF16)
    count = n_ctx // 2
    odd = position % 2
    gateup_grad = jnp.zeros((quarter, 2, n_far, share), BF16)
    for flip in range(2):
        for step in range(n_far):
            to_far = (far + step) % n_far
            part = lax.dynamic_index_in_dim(gu_sum, to_far, 0, False)
            which = odd ^ flip
            part = jnp.where(which == 0, part[:, :share], part[:, share:])
            pairs = []
            for c in range(n_ctx):
                for f in range(n_far):
                    pairs.append((c * n_far + f, (((c % 2) ^ flip) * count + c // 2) * n_far + (f + step) % n_far))
            came = lax.ppermute(part, GROUP, pairs)
            side = (position // count) ^ flip
            source_far = (far - step) % n_far
            gateup_grad = lax.dynamic_update_slice(
                gateup_grad, came[:, None, None], (0, side, source_far, 0)
            )
    gateup_grad = gateup_grad.reshape(quarter, 2 * n_far * share).astype(F32)
    down_grad = down_grad.reshape(share, n_far, n_near, width // n_seq)
    theirs = lax.dynamic_index_in_dim(down_grad, 1 - near, 2, False)
    mine = lax.dynamic_index_in_dim(down_grad, near, 2, False)
    down_sum = (mine.astype(F32) + swap(theirs, "near").astype(F32)).astype(BF16)
    down_sum = exchange(down_sum.transpose(1, 0, 2), ("far",))
    down_grad = down_sum.reshape(n_far * share, width // n_seq).astype(F32)

    d_middle_norm, d_gain2 = norm_backward(d_hidden2, normed2, scale2, gain2)
    d_middle = d_final.astype(F32) + d_middle_norm
    d_bias = jnp.sum(d_middle, axis=0)
    d_low = d_middle.astype(BF16)
    d_mixed = dot_last(d_low, full_out).astype(BF16).reshape(block_len, NH, HD)
    scores = jnp.einsum("qhd,kd->hqk", query, key, preferred_element_type=F32)
    scores = jnp.where(allowed[None], scores, NEG)
    probs = jnp.exp(scores - log_total)
    probs_again = probs.astype(BF16)
    d_probs = jnp.einsum("qhd,kd->hqk", d_mixed, value, preferred_element_type=F32)
    delta = jnp.sum(probs * d_probs, axis=-1, keepdims=True)
    d_scores = (probs * (d_probs - delta)).astype(BF16)
    d_query = jnp.einsum("hqk,kd->qhd", d_scores, key, preferred_element_type=F32) * q_scale
    d_key = jnp.einsum("hqk,qhd->kd", d_scores, query, preferred_element_type=F32)
    d_value = jnp.einsum("hqk,qhd->kd", probs_again, d_mixed, preferred_element_type=F32)
    d_query = d_query.reshape(block_len, n_ctx, q_cols).astype(BF16).transpose(1, 0, 2)
    d_query = exchange(d_query, CTX).reshape(length, q_cols)
    d_keyval = jnp.concatenate([d_key, d_value], axis=1).astype(BF16)
    d_keyval = exchange(d_keyval.reshape(length, n_ctx, kv_cols).transpose(1, 0, 2), CTX)
    d_keyval = jnp.sum(d_keyval.astype(F32), axis=0).astype(BF16)
    d_qkv = jnp.concatenate([d_query, d_keyval], axis=1)
    d_hidden1 = scatter_ctx(dot_last(d_qkv, w_qkv).astype(BF16).reshape(n_ctx, block_len, width))
    scale1 = norm_scale(residual)
    d_input_norm, d_gain1 = norm_backward(d_hidden1, residual * scale1, scale1, gain1)
    d_input = d_middle + d_input_norm

    qkv_grad = lax.psum_scatter(
        dot_first(hidden1, d_qkv).astype(BF16), SEQ, scatter_dimension=0, tiled=True
    ).astype(F32)
    low_rows = gather_ctx(d_low).reshape(length, width)
    mixed_cols = exchange(mixed.reshape(block_len, n_ctx, q_cols).transpose(1, 0, 2), CTX)
    mixed_cols = mixed_cols.reshape(length, q_cols)
    out_grad = lax.psum_scatter(
        dot_first(mixed_cols, low_rows).astype(BF16), SEQ, scatter_dimension=1, tiled=True
    ).astype(F32)
    sums = jnp.stack([d_gain1, d_bias, d_gain2]).reshape(3, n_all, rows).transpose(1, 0, 2)
    sums = jnp.sum(exchange(sums, EVERY), axis=0)
    return (
        output.reshape(1, block_len, width),
        d_input.reshape(1, block_len, width),
        sums[0],
        qkv_grad[:, :q_cols],
        qkv_grad[:, q_cols:],
        out_grad,
        sums[1],
        sums[2],
        gateup_grad,
        down_grad,
    )


def solution(mesh):
    n_ctx, n_seq = mesh.shape["ctx"], mesh.shape["seq"]
    side = math.isqrt(n_ctx // 2)
    fine = Mesh(
        mesh.devices.reshape(n_ctx // 2 // side, side, 2, n_seq // 2, 2), EVERY
    )
    whole = P(EVERY)
    return jax.shard_map(
        per_device,
        mesh=fine,
        in_specs=(
            P(SEQ, CTX, None),
            P(SEQ, CTX, None),
            whole,
            whole,
            whole,
            whole,
            whole,
            whole,
            whole,
            whole,
        ),
        out_specs=(
            P(SEQ, CTX, None),
            P(SEQ, CTX, None),
            whole,
            P(SEQ, CTX),
            P(SEQ, CTX),
            P(CTX, SEQ),
            whole,
            whole,
            P(SEQ, CTX),
            P(CTX, SEQ),
        ),
        check_vma=False,
    )
```

```python
import functools
import math

import jax
import jax.numpy as jnp
from jax import lax
from jax.experimental import pallas as pl
from jax.experimental.pallas import tpu as pltpu
from jax.sharding import Mesh, PartitionSpec as P

NH = 10
HD = 256
FF = 7680
WINDOW = 2048

EPS = 1e-06
NEG = -1e30

F32 = jnp.float32
BF16 = jnp.bfloat16

CTX = ("hi", "lo", "core")
GROUP = ("hi", "lo", "core", "far")
SEQ = ("far", "near")
EVERY = ("hi", "lo", "core", "far", "near")


def dot(left, right):
    return jnp.dot(left, right, preferred_element_type=F32)


def dot_last(left, right):
    return lax.dot_general(left, right, (((1,), (1,)), ((), ())), preferred_element_type=F32)


def dot_first(left, right):
    return lax.dot_general(left, right, (((0,), (0,)), ((), ())), preferred_element_type=F32)


def send(value, axis, step):
    count = lax.axis_size(axis)
    return lax.ppermute(value, axis, [(i, (i + step) % count) for i in range(count)])


def meet(*values):
    return lax.optimization_barrier(values)


def side():
    return lax.axis_size("lo")


def send_cross(value, step, second):
    k = side()
    pairs = []
    for h in range(k):
        for l in range(k):
            for c in range(2):
                along_lo = (c == 0) != second
                to_h, to_l = (h, (l + step) % k) if along_lo else ((h + step) % k, l)
                pairs.append(((h * k + l) * 2 + c, (to_h * k + to_l) * 2 + c))
    return lax.ppermute(value, CTX, pairs)


def gather_0(block):
    return jnp.concatenate([block, send(block, "core", 1)])


def gather_1(pair):
    return [send_cross(pair, i, False) for i in range(1, side())]


def gather_2(sides):
    rows = sides[0].shape[0] // 2
    return [send_cross(value[:rows], j, True) for value in sides for j in range(1, side())]


def gather_3(pair, sides, corners):
    own = jnp.concatenate(sides + corners)
    return own, send(own, "core", 1)


def gather_all(pair, halves):
    rows = pair.shape[0] // 2
    return jnp.concatenate([pair[:rows], halves[0], pair[rows:], halves[1]])


def add(*values):
    return sum((value.astype(F32) for value in values[1:]), values[0].astype(F32))


def block_of(value, at, rows):
    k = side()
    value = value.reshape(-1, k * k, rows, value.shape[-1])[:, at]
    return value.reshape(-1, value.shape[-1])


def scatter_1(keep, came, rows):
    k = side()
    back = []
    for i in range(k - 1):
        for j in range(1, k):
            at = 2 * k - 1 + i * (k - 1) + j - 1
            low = add(block_of(keep, at, rows), block_of(came, at, rows)).astype(BF16)
            back.append(send_cross(low, -j, True))
    return back


def scatter_2(keep, came, back, rows):
    k = side()
    sides = []
    for i in range(1, k):
        first = add(block_of(keep, 2 * i - 1, rows), block_of(came, 2 * i - 1, rows))
        first = add(first, *back[(i - 1) * (k - 1) : i * (k - 1)])
        second = add(block_of(keep, 2 * i, rows), block_of(came, 2 * i, rows))
        sides.append(send_cross(jnp.concatenate([first, second]).astype(BF16), -i, False))
    return sides


def scatter_3(sides):
    half = sides[0].shape[0] // 2
    return send(add(*[value[half:] for value in sides]).astype(BF16), "core", 1)


def scatter_4(keep, came, sides, other, rows):
    half = sides[0].shape[0] // 2
    return add(
        block_of(keep, 0, rows), block_of(came, 0, rows), other, *[value[:half] for value in sides]
    )


def copy_blocks(order_ref, from_ref, to_ref):
    for n in range(to_ref.shape[0]):
        to_ref[n] = from_ref[order_ref[n]]


def pick_blocks(blocks, order):
    shape = order.shape + blocks.shape[1:]
    return pl.pallas_call(
        copy_blocks,
        out_shape=jax.ShapeDtypeStruct(shape, blocks.dtype),
        in_specs=[pl.BlockSpec(memory_space=pltpu.SMEM), pl.BlockSpec(memory_space=pltpu.VMEM)],
        out_specs=pl.BlockSpec(memory_space=pltpu.VMEM),
        cost_estimate=pl.CostEstimate(
            flops=0, bytes_accessed=2 * blocks.size * blocks.dtype.itemsize, transcendentals=0
        ),
        name="pick_blocks",
    )(order, blocks)


def order_ctx(by_device):
    k = side()
    h, l, c = (lax.axis_index(axis) for axis in CTX)
    picked = []
    for n in range(2 * k * k):
        if by_device:
            ih, il, ic = n // (2 * k), n // 2 % k, n % 2
            dh, dl = (h - ih) % k, (l - il) % k
            on_lo, on_hi = (dh == 0) & (dl != 0), (dl == 0) & (dh != 0)
            charge = jnp.where(on_lo, 0, jnp.where(on_hi, 1, ic))
            i, j = (dl, dh) if ic == 0 else (dh, dl)
            at = 2 * k - 1 + (i - 1) * (k - 1) + j - 1
            at = jnp.where(on_lo, 2 * dl - 1 + (ic != 0), jnp.where(on_hi, 2 * dh - 1 + (ic != 1), at))
            at = jnp.where((dh == 0) & (dl == 0), 0, at)
            source = jnp.where(charge == c, 0, k * k) + at
        else:
            other, at = n // (k * k), n % (k * k)
            charge = c ^ other
            if at == 0:
                i, j, core = 0, 0, charge
            elif at < 2 * k - 1:
                i, j, core = (at + 1) // 2, 0, charge ^ ((at + 1) % 2)
            else:
                i, j, core = (at - 2 * k + 1) // (k - 1) + 1, (at - 2 * k + 1) % (k - 1) + 1, charge
            dh, dl = jnp.where(charge == 0, j, i), jnp.where(charge == 0, i, j)
            source = ((h - dh) % k * k + (l - dl) % k) * 2 + core
        picked.append(source)
    return jnp.stack(picked).astype(jnp.int32)


def exchange(value, axes):
    return lax.all_to_all(value, axes, split_axis=0, concat_axis=0, tiled=True)


def dot_rows(left, right):
    return lax.dot_general(left, right, (((1,), (1,)), ((), ())), preferred_element_type=F32)


def middle_kernel(
    share, wide, order_ref, hidden_ref, d_first_ref, d_second_ref, gate_ref, up_ref, inner_ref, d_gu_ref, keep_ref, give_ref
):
    hidden = hidden_ref[...]
    gate = jnp.dot(hidden, gate_ref[...], preferred_element_type=F32)
    up = jnp.dot(hidden, up_ref[...], preferred_element_type=F32)
    d_inner = jnp.concatenate([d_first_ref[0], d_second_ref[0]]).astype(F32)
    root = (2.0 / math.pi) ** 0.5
    square = gate * gate
    bent = jnp.tanh(root * gate * (1.0 + 0.044715 * square))
    half = 0.5 * (1.0 + bent)
    gelu = gate * half
    slope = half + 0.5 * gate * (1.0 - bent * bent) * (root * (1.0 + 3 * 0.044715 * square))
    d_gate = (d_inner * up * slope).astype(BF16)
    d_up = (d_inner * gelu).astype(BF16)
    inner_ref[:, :share] = (gelu * up).astype(BF16)
    d_gu_ref[:, :share] = d_gate
    d_gu_ref[:, wide : wide + share] = d_up
    if wide > share:
        rest = jnp.zeros((hidden.shape[0], wide - share), BF16)
        inner_ref[:, share:] = rest
        d_gu_ref[:, share:wide] = rest
        d_gu_ref[:, wide + share :] = rest
    back = (dot_rows(d_gate, gate_ref[...]) + dot_rows(d_up, up_ref[...])).astype(BF16)
    step, steps = pl.program_id(0), pl.num_programs(0)

    @pl.when(step < steps // 2)
    def _():
        keep_ref[...] = back

    @pl.when(step >= steps // 2)
    def _():
        give_ref[...] = back


def feed_forward(hidden, d_inner, order, w_gate, w_up, wide):
    length, width = hidden.shape
    block, share = d_inner.shape[1:]
    rows = 2 * block
    steps = length // rows
    weight = pl.BlockSpec((width, share), lambda n, order_ref: (0, 0), pipeline_mode=pl.Buffered(1))
    return pl.pallas_call(
        functools.partial(middle_kernel, share, wide),
        out_shape=(
            jax.ShapeDtypeStruct((length, wide), BF16),
            jax.ShapeDtypeStruct((length, 2 * wide), BF16),
            jax.ShapeDtypeStruct((length // 2, width), BF16),
            jax.ShapeDtypeStruct((length // 2, width), BF16),
        ),
        grid_spec=pltpu.PrefetchScalarGridSpec(
            num_scalar_prefetch=1,
            grid=(steps,),
            in_specs=[
                pl.BlockSpec((rows, width), lambda n, order_ref: (n, 0)),
                pl.BlockSpec((1, block, share), lambda n, order_ref: (order_ref[2 * n], 0, 0)),
                pl.BlockSpec((1, block, share), lambda n, order_ref: (order_ref[2 * n + 1], 0, 0)),
                weight,
                weight,
            ],
            out_specs=[
                pl.BlockSpec((rows, wide), lambda n, order_ref: (n, 0)),
                pl.BlockSpec((rows, 2 * wide), lambda n, order_ref: (n, 0)),
                pl.BlockSpec((rows, width), lambda n, order_ref: (jnp.minimum(n, steps // 2 - 1), 0)),
                pl.BlockSpec((rows, width), lambda n, order_ref: (jnp.maximum(n - steps // 2, 0), 0)),
            ],
        ),
        compiler_params=pltpu.CompilerParams(vmem_limit_bytes=48 * 2**20),
        cost_estimate=pl.CostEstimate(
            flops=8 * length * width * share,
            bytes_accessed=4 * length * width + 4 * width * share,
            transcendentals=length * share,
        ),
        name="feed_forward",
    )(order, hidden, d_inner, d_inner, w_gate, w_up)


def norm_scale(value):
    return lax.rsqrt(jnp.mean(value * value, axis=-1, keepdims=True) + EPS)


def norm_backward(d_normed, normed, scale):
    return scale * (d_normed - normed * jnp.mean(d_normed * normed, axis=-1, keepdims=True))


def with_gain(weight, gain):
    return (weight.astype(F32) * gain.astype(F32)[:, None]).astype(BF16)


def in_place(mine, other, at):
    both = jnp.zeros(mine.shape[:1] + (2,) + mine.shape[1:], mine.dtype)
    rest = (0,) * (mine.ndim - 1)
    both = lax.dynamic_update_slice(both, mine[:, None], (0, at) + rest)
    return lax.dynamic_update_slice(both, other[:, None], (0, 1 - at) + rest)


def per_device(
    tokens, cotangent, gain_attn, w_query, w_keyval, w_out, b_out, gain_ffn, w_gateup, w_down
):
    block_len, width = tokens.shape[1:]
    n_ctx = lax.axis_size("hi") * lax.axis_size("lo") * lax.axis_size("core")
    n_far, n_near = lax.axis_size("far"), lax.axis_size("near")
    n_seq = n_far * n_near
    n_all = n_ctx * n_seq
    n_group = n_ctx * n_far
    rows = w_query.shape[0]
    length = n_ctx * block_len
    q_scale = HD ** (-0.5)
    position = (lax.axis_index("hi") * lax.axis_size("lo") + lax.axis_index("lo")) * 2 + lax.axis_index("core")
    far, near = lax.axis_index("far"), lax.axis_index("near")
    q_cols = NH * HD // n_ctx
    kv_cols = 2 * HD // n_ctx
    share = FF // n_group
    quarter = width // n_seq

    block = tokens.reshape(block_len, width)
    d_final = cotangent.reshape(block_len, width)
    residual = block.astype(F32)

    qkv_send = jnp.concatenate(
        [
            with_gain(w_query, gain_attn).reshape(rows, n_ctx, q_cols),
            with_gain(w_keyval, gain_attn).reshape(rows, n_ctx, kv_cols),
        ],
        axis=2,
    ).transpose(1, 0, 2)
    qkv_send = jnp.broadcast_to(qkv_send[:, None], (n_ctx, n_seq) + qkv_send.shape[1:])
    scale1 = norm_scale(residual)
    normed1 = residual * scale1
    vectors = jnp.stack([gain_attn, b_out, gain_ffn])
    vectors = jnp.pad(vectors, ((0, 13), (0, width - rows)))
    out_send = jnp.concatenate([w_out, vectors])[None]
    out_near = send(out_send, "near", 1)
    out_far = send(out_send, "far", 1)
    out_both = lax.ppermute(out_send, SEQ, [(i, (i + n_near) % n_seq ^ 1) for i in range(n_seq)])
    hidden1 = lax.all_gather(normed1.astype(BF16), CTX, axis=0, tiled=True)
    w_qkv = exchange(qkv_send.reshape((n_all,) + qkv_send.shape[2:]), EVERY)
    gateup_send = with_gain(w_gateup, gain_ffn).reshape(rows, 2, n_group, share).transpose(1, 2, 0, 3)

    hidden1, w_qkv, gateup_send, out_near, out_far, out_both, d_start = meet(
        hidden1,
        w_qkv.reshape(width, q_cols + kv_cols),
        gateup_send,
        out_near,
        out_far,
        out_both,
        d_final,
    )
    gate_half = exchange(gateup_send[0], GROUP)
    f_theirs = send(d_start, "far", 1)

    def along_seq(part):
        mine = in_place(part(out_send), part(out_near), near)
        other = in_place(part(out_far), part(out_both), near)
        return in_place(mine, other, far)

    out_rows = along_seq(lambda value: value[:, :rows]).reshape(n_seq * rows, width)
    vectors = along_seq(lambda value: value[:, rows : rows + 3, :rows]).reshape(-1)
    full_out = lax.all_gather(out_rows, CTX, axis=0, tiled=True)
    down_other = send(w_down, "near", 1)

    qkv = dot(hidden1, w_qkv)
    qkv = jnp.concatenate([qkv[:, :q_cols] * q_scale, qkv[:, q_cols:]], axis=1).astype(BF16)
    qkv = qkv.reshape(n_ctx, block_len, q_cols + kv_cols)
    kv_send = qkv[:, :, q_cols:].transpose(1, 0, 2).reshape(block_len, 2 * HD)
    kv_send = jnp.broadcast_to(kv_send[None], (n_ctx, block_len, 2 * HD))
    spare = block_len * 8 - n_seq * 3 * rows
    extra = jnp.concatenate([vectors, jnp.zeros((spare,), BF16)]).reshape(1, block_len, 8)
    extra = jnp.broadcast_to(extra, (n_ctx, block_len, 8))
    q_send = jnp.concatenate([qkv[:, :, :q_cols], kv_send, extra], axis=2)
    q_send, gate_half = meet(q_send, gate_half)
    came = exchange(q_send, CTX)
    gate_other = send(gate_half, "near", 1)
    came, up_send = meet(came, gateup_send[1])
    up_half = exchange(up_send, GROUP)
    vectors = came[:, :, q_cols + 2 * HD :].reshape(n_ctx, -1)[:, : n_seq * 3 * rows]
    vectors = vectors.reshape(n_ctx * n_seq, 3, rows).transpose(1, 0, 2).reshape(3, width).astype(F32)
    gain1, bias, gain2 = vectors[0], vectors[1], vectors[2]
    query = came[:, :, :q_cols].transpose(1, 0, 2).reshape(block_len, NH, HD)
    keyval = came[:, :, q_cols : q_cols + 2 * HD].reshape(n_ctx, block_len, n_ctx, kv_cols).transpose(2, 1, 0, 3)
    keyval = keyval.reshape(length, 2 * HD)
    key, value = keyval[:, :HD], keyval[:, HD:]
    spacing = (position * block_len + jnp.arange(block_len, dtype=jnp.int32))[:, None] - jnp.arange(
        length, dtype=jnp.int32
    )[None, :]
    allowed = (spacing >= 0) & (spacing < WINDOW)
    scores = jnp.einsum("qhd,kd->hqk", query, key, preferred_element_type=F32)
    scores = jnp.where(allowed[None], scores, NEG)
    maximum = jnp.max(scores, axis=-1, keepdims=True)
    log_total = maximum + jnp.log(jnp.sum(jnp.exp(scores - maximum), axis=-1, keepdims=True))
    probs_low = jnp.exp(scores - log_total).astype(BF16)
    mixed = jnp.einsum("hqk,kd->qhd", probs_low, value, preferred_element_type=F32).astype(BF16)
    mixed = mixed.reshape(block_len, NH * HD)

    mixed, f_theirs, full_out, gate_other = meet(mixed, f_theirs, full_out, gate_other)
    final_rows = lax.all_gather(jnp.concatenate([d_start, f_theirs]), CTX, axis=0, tiled=True)
    middle = residual + dot(mixed, full_out) + bias

    scale2 = norm_scale(middle)
    normed2 = middle * scale2
    hidden2 = normed2.astype(BF16)
    m_pair = gather_0(hidden2)
    theirs = send(hidden2, "far", 1)
    m_sides = gather_1(m_pair)
    m_sides, theirs, up_half = meet(m_sides, theirs, up_half)
    up_other = send(up_half, "near", 1)
    m_corners = gather_2(m_sides)
    t_pair = gather_0(theirs)
    w_dn = in_place(w_down[None], down_other[None], near).reshape(share, width)
    devices = order_ctx(False)
    d_inner = dot_last(final_rows, w_dn).astype(BF16).reshape(2 * n_ctx, block_len, share)
    m_corners, t_pair, d_inner = meet(m_corners, t_pair, d_inner)
    m_halves = gather_3(m_pair, m_sides, m_corners)
    t_sides = gather_1(t_pair)
    m_halves, t_sides, up_other = meet(m_halves, t_sides, up_other)
    t_corners = gather_2(t_sides)
    hidden_m = gather_all(m_pair, m_halves)
    w_gate = in_place(gate_half, gate_other, near).reshape(width, share)
    t_halves = gather_3(t_pair, t_sides, t_corners)
    w_up = in_place(up_half, up_other, near).reshape(width, share)

    wide = -(-share // 128) * 128
    half = length // 2
    mixed_send = mixed.reshape(block_len, n_ctx, q_cols).transpose(1, 0, 2)
    mixed_send, t_halves = meet(mixed_send, t_halves)
    mixed_cols = exchange(mixed_send, CTX)
    inner_m, d_gu_m, m_keep, m_give = feed_forward(hidden_m, d_inner, 2 * devices, w_gate, w_up, wide)
    m_give, t_halves = meet(m_give, t_halves)
    m_came = send(m_give, "core", 1)
    hidden_t = gather_all(t_pair, t_halves)
    inner_t, d_gu_t, t_keep, t_give = feed_forward(hidden_t, d_inner, 2 * devices + 1, w_gate, w_up, wide)
    t_give, m_keep, m_came, mixed_cols = meet(t_give, m_keep, m_came, mixed_cols)
    t_came = send(t_give, "core", 1)
    m_back = scatter_1(m_keep, m_came, block_len)

    gu_grad = dot_first(hidden_m, d_gu_m)
    gu_grad, t_keep, t_came, m_back, m_keep, m_came = meet(gu_grad, t_keep, t_came, m_back, m_keep, m_came)
    t_back = scatter_1(t_keep, t_came, block_len)
    m_sides = scatter_2(m_keep, m_came, m_back, block_len)
    gu_grad = (gu_grad + dot_first(hidden_t, d_gu_t)).astype(BF16)
    gu_grad, t_back, t_keep, t_came = meet(gu_grad, t_back, t_keep, t_came)
    t_sides = scatter_2(t_keep, t_came, t_back, block_len)
    mixed_cols = pick_blocks(mixed_cols, devices).reshape(length, q_cols)
    places = order_ctx(True)
    inner_rows = jnp.concatenate([inner_m, inner_t]).reshape(2 * n_ctx, block_len, wide)
    inner_rows = pick_blocks(inner_rows, jnp.stack([places, places + n_ctx], axis=1).reshape(-1))
    down_grad = dot_first(final_rows, inner_rows.reshape(2 * length, wide)).astype(BF16)
    down_grad, t_sides, m_sides, mixed_cols = meet(down_grad, t_sides, m_sides, mixed_cols)
    t_other = scatter_3(t_sides)
    m_other = scatter_3(m_sides)
    ffn_grad = [value.reshape(n_far, n_near, quarter, -1) for value in (gu_grad, down_grad)]
    ffn_grad = jnp.stack(
        [jnp.concatenate([value[:, n] for value in ffn_grad], axis=2) for n in range(n_near)]
    )
    ffn_grad, t_other, t_keep, t_came, t_sides = meet(ffn_grad, t_other, t_keep, t_came, t_sides)
    ffn_grad = lax.psum_scatter(ffn_grad, "near", scatter_dimension=0, tiled=True)
    theirs = scatter_4(t_keep, t_came, t_sides, t_other, block_len).astype(BF16)
    theirs = send(theirs, "far", 1)
    out_give = dot(jnp.concatenate([inner_m[half:, :share], inner_t[half:, :share]]), w_dn).astype(BF16)
    out_keep = dot(jnp.concatenate([inner_m[:half, :share], inner_t[:half, :share]]), w_dn).astype(BF16)
    m_other, theirs, out_keep, out_give = meet(m_other, theirs, out_keep, out_give)
    d_hidden2 = scatter_4(m_keep, m_came, m_sides, m_other, block_len) + theirs.astype(F32)

    d_middle = d_final.astype(F32) + norm_backward(d_hidden2, normed2, scale2)
    d_gain2 = jnp.sum(d_hidden2 * normed2, axis=0) / gain2
    d_bias = jnp.sum(d_middle, axis=0)
    d_low = d_middle.astype(BF16)
    d_low, out_give = meet(d_low, out_give)
    l_pair = gather_0(d_low)
    l_pair, d_low, out_give = meet(l_pair, d_low, out_give)
    l_sides = gather_1(l_pair)
    o_came = send(out_give, "core", 1)
    d_mixed = dot_last(d_low, full_out).astype(BF16)
    d_mixed, o_came = meet(d_mixed, o_came)
    o_back = scatter_1(out_keep, o_came, block_len)
    d_mixed = d_mixed.reshape(block_len, NH, HD)
    scores = jnp.einsum("qhd,kd->hqk", query, key, preferred_element_type=F32)
    scores = jnp.where(allowed[None], scores, NEG)
    probs = jnp.exp(scores - log_total)
    probs_again = probs.astype(BF16)
    d_probs = jnp.einsum("qhd,kd->hqk", d_mixed, value, preferred_element_type=F32)
    delta = jnp.sum(probs * d_probs, axis=-1, keepdims=True)
    d_scores = (probs * (d_probs - delta)).astype(BF16)
    d_query = jnp.einsum("hqk,kd->qhd", d_scores, key, preferred_element_type=F32) * q_scale
    d_key = jnp.einsum("hqk,qhd->kd", d_scores, query, preferred_element_type=F32)
    d_value = jnp.einsum("hqk,qhd->kd", probs_again, d_mixed, preferred_element_type=F32)
    d_query = d_query.reshape(block_len, n_ctx, q_cols).astype(BF16).transpose(1, 0, 2)
    d_keyval = jnp.concatenate([d_key, d_value], axis=1).astype(BF16)
    d_keyval = d_keyval.reshape(n_ctx, block_len, n_ctx, kv_cols).transpose(2, 1, 0, 3)
    d_keyval = d_keyval.reshape(n_ctx, block_len, 2 * HD)
    d_send = jnp.concatenate([d_query, d_keyval], axis=2)
    d_send, l_sides, o_back, out_keep, o_came = meet(d_send, l_sides, o_back, out_keep, o_came)
    came = exchange(d_send, CTX)
    l_corners = gather_2(l_sides)
    o_sides = scatter_2(out_keep, o_came, o_back, block_len)
    came, l_corners, ffn_grad = meet(came, l_corners, ffn_grad)
    ffn_grad = ffn_grad[0]
    own_rows = lax.dynamic_index_in_dim(ffn_grad, far, 0, False)
    give = lax.dynamic_index_in_dim(ffn_grad, (far + 1) % n_far, 0, False)
    came, give = meet(came, give)
    by_far = lax.all_gather(give, "far", axis=0)
    l_halves = gather_3(l_pair, l_sides, l_corners)
    d_keyval = jnp.sum(came[:, :, q_cols:].astype(F32), axis=0).astype(BF16)
    d_keyval = d_keyval.reshape(block_len, n_ctx, kv_cols).transpose(1, 0, 2)
    d_qkv = jnp.concatenate([came[:, :, :q_cols], d_keyval], axis=2)
    d_back = pick_blocks(d_qkv, devices).reshape(length, q_cols + kv_cols)
    d_qkv = d_qkv.reshape(length, q_cols + kv_cols)
    e_came = send(dot_last(d_back[half:], w_qkv).astype(BF16), "core", 1)
    e_keep = dot_last(d_back[:half], w_qkv).astype(BF16)
    e_keep, e_came, l_halves, o_sides, d_qkv = meet(e_keep, e_came, l_halves, o_sides, d_qkv)
    e_back = scatter_1(e_keep, e_came, block_len)
    o_other = scatter_3(o_sides)
    out_grad = dot_first(gather_all(l_pair, l_halves), mixed_cols)
    qkv_grad = dot_first(hidden1, d_qkv)
    d_gain1 = jnp.sum(qkv_grad * w_qkv.astype(F32), axis=1) / gain1
    attn_grad = jnp.concatenate([qkv_grad.astype(BF16), out_grad.astype(BF16)], axis=1)
    e_back, o_other, out_keep, o_came = meet(e_back, o_other, out_keep, o_came)
    e_sides = scatter_2(e_keep, e_came, e_back, block_len)
    sums = jnp.stack([d_gain1, d_bias, d_gain2]).reshape(3, n_all, rows).transpose(1, 0, 2)
    e_sides, attn_grad, sums = meet(e_sides, attn_grad, sums)
    attn_grad = lax.psum_scatter(attn_grad, SEQ, scatter_dimension=0, tiled=True).astype(F32)
    e_other = scatter_3(e_sides)
    o_total = scatter_4(out_keep, o_came, o_sides, o_other, block_len)
    o_theirs = send(o_total[block_len:].astype(BF16), "far", 1)
    e_other, o_theirs, by_far, sums = meet(e_other, o_theirs, by_far, sums)
    sums = exchange(sums, EVERY)
    d_normed1 = scatter_4(e_keep, e_came, e_sides, e_other, block_len)
    d_input = d_middle + norm_backward(d_normed1, normed1, scale1)
    output = (middle + o_total[:block_len] + o_theirs.astype(F32)).astype(BF16)
    count = n_ctx // 2
    odd = position % 2
    by_far = [jnp.where(far == f, own_rows, by_far[f]) for f in range(n_far)]
    gate, up = [jnp.stack([v[:, at : at + wide] for v in by_far]) for at in (0, wide)]
    pieces = []
    for flip in range(2):
        pairs = [(c, ((c % 2) ^ flip) * count + c // 2) for c in range(n_ctx)]
        pieces.append(lax.ppermute(jnp.where(odd == flip, gate, up), CTX, pairs))
    down_grad = jnp.concatenate(
        [value[:, 2 * wide : 2 * wide + share].T.astype(F32) for value in by_far]
    )
    upper = position >= count
    columns = [jnp.where(upper, pieces[1], pieces[0]), jnp.where(upper, pieces[0], pieces[1])]
    own_gain = lax.dynamic_slice_in_dim(gain2, (far * n_near + near) * quarter, quarter)
    gateup_grad = (
        jnp.concatenate([columns[i][f][:, :share] for i in range(2) for f in range(n_far)], axis=1).astype(F32)
        * own_gain[:, None]
    )
    attn_grad, sums = meet(attn_grad, sums)
    sums = jnp.sum(sums, axis=0)
    own_gain = lax.dynamic_slice_in_dim(gain1, (far * n_near + near) * quarter, quarter)
    qkv_grad = attn_grad[:, : q_cols + kv_cols] * own_gain[:, None]
    out_grad = attn_grad[:, q_cols + kv_cols :].T
    return (
        output.reshape(1, block_len, width),
        d_input.reshape(1, block_len, width),
        sums[0],
        qkv_grad[:, :q_cols],
        qkv_grad[:, q_cols:],
        out_grad,
        sums[1],
        sums[2],
        gateup_grad,
        down_grad,
    )


def solution(mesh):
    n_ctx, n_seq = mesh.shape["ctx"], mesh.shape["seq"]
    side = math.isqrt(n_ctx // 2)
    fine = Mesh(
        mesh.devices.reshape(n_ctx // 2 // side, side, 2, n_seq // 2, 2), EVERY
    )
    whole = P(EVERY)
    return jax.shard_map(
        per_device,
        mesh=fine,
        in_specs=(
            P(SEQ, CTX, None),
            P(SEQ, CTX, None),
            whole,
            whole,
            whole,
            whole,
            whole,
            whole,
            whole,
            whole,
        ),
        out_specs=(
            P(SEQ, CTX, None),
            P(SEQ, CTX, None),
            whole,
            P(SEQ, CTX),
            P(SEQ, CTX),
            P(CTX, SEQ),
            whole,
            whole,
            P(SEQ, CTX),
            P(CTX, SEQ),
        ),
        check_vma=False,
    )
```

```python
import functools
import math

import jax
import jax.numpy as jnp
from jax import lax
from jax.experimental import pallas as pl
from jax.experimental.pallas import tpu as pltpu
from jax.sharding import Mesh, PartitionSpec as P

NH = 10
HD = 256
FF = 7680
WINDOW = 2048

EPS = 1e-06
NEG = -1e30

F32 = jnp.float32
BF16 = jnp.bfloat16

CTX = ("hi", "lo", "core")
GROUP = ("hi", "lo", "core", "far")
SEQ = ("far", "near")
EVERY = ("hi", "lo", "core", "far", "near")


def dot(left, right):
    return jnp.dot(left, right, preferred_element_type=F32)


def dot_last(left, right):
    return lax.dot_general(left, right, (((1,), (1,)), ((), ())), preferred_element_type=F32)


def dot_first(left, right):
    return lax.dot_general(left, right, (((0,), (0,)), ((), ())), preferred_element_type=F32)


def send(value, axis, step):
    count = lax.axis_size(axis)
    return lax.ppermute(value, axis, [(i, (i + step) % count) for i in range(count)])


def meet(*values):
    return lax.optimization_barrier(values)


def side():
    return lax.axis_size("lo")


def send_cross(value, step, second):
    k = side()
    pairs = []
    for h in range(k):
        for l in range(k):
            for c in range(2):
                along_lo = (c == 0) != second
                to_h, to_l = (h, (l + step) % k) if along_lo else ((h + step) % k, l)
                pairs.append(((h * k + l) * 2 + c, (to_h * k + to_l) * 2 + c))
    return lax.ppermute(value, CTX, pairs)


def gather_0(block):
    return jnp.concatenate([block, send(block, "core", 1)])


def gather_1(pair):
    return [send_cross(pair, i, False) for i in range(1, side())]


def gather_2(sides):
    rows = sides[0].shape[0] // 2
    return [send_cross(value[:rows], j, True) for value in sides for j in range(1, side())]


def gather_3(pair, sides, corners):
    own = jnp.concatenate(sides + corners)
    return own, send(own, "core", 1)


def gather_all(pair, halves):
    rows = pair.shape[0] // 2
    return jnp.concatenate([pair[:rows], halves[0], pair[rows:], halves[1]])


def add(*values):
    return sum((value.astype(F32) for value in values[1:]), values[0].astype(F32))


def block_of(value, at, rows):
    k = side()
    value = value.reshape(-1, k * k, rows, value.shape[-1])[:, at]
    return value.reshape(-1, value.shape[-1])


def scatter_1(keep, came, rows):
    k = side()
    back = []
    for i in range(k - 1):
        for j in range(1, k):
            at = 2 * k - 1 + i * (k - 1) + j - 1
            low = add(block_of(keep, at, rows), block_of(came, at, rows)).astype(BF16)
            back.append(send_cross(low, -j, True))
    return back


def scatter_2(keep, came, back, rows):
    k = side()
    sides = []
    for i in range(1, k):
        first = add(block_of(keep, 2 * i - 1, rows), block_of(came, 2 * i - 1, rows))
        first = add(first, *back[(i - 1) * (k - 1) : i * (k - 1)])
        second = add(block_of(keep, 2 * i, rows), block_of(came, 2 * i, rows))
        sides.append(send_cross(jnp.concatenate([first, second]).astype(BF16), -i, False))
    return sides


def scatter_3(sides):
    half = sides[0].shape[0] // 2
    return send(add(*[value[half:] for value in sides]).astype(BF16), "core", 1)


def scatter_4(keep, came, sides, other, rows):
    half = sides[0].shape[0] // 2
    return add(
        block_of(keep, 0, rows), block_of(came, 0, rows), other, *[value[:half] for value in sides]
    )


def copy_blocks(order_ref, from_ref, to_ref):
    for n in range(to_ref.shape[0]):
        to_ref[n] = from_ref[order_ref[n]]


def pick_blocks(blocks, order):
    shape = order.shape + blocks.shape[1:]
    return pl.pallas_call(
        copy_blocks,
        out_shape=jax.ShapeDtypeStruct(shape, blocks.dtype),
        in_specs=[pl.BlockSpec(memory_space=pltpu.SMEM), pl.BlockSpec(memory_space=pltpu.VMEM)],
        out_specs=pl.BlockSpec(memory_space=pltpu.VMEM),
        cost_estimate=pl.CostEstimate(
            flops=0, bytes_accessed=2 * blocks.size * blocks.dtype.itemsize, transcendentals=0
        ),
        name="pick_blocks",
    )(order, blocks)


def order_ctx(by_device):
    k = side()
    h, l, c = (lax.axis_index(axis) for axis in CTX)
    picked = []
    for n in range(2 * k * k):
        if by_device:
            ih, il, ic = n // (2 * k), n // 2 % k, n % 2
            dh, dl = (h - ih) % k, (l - il) % k
            on_lo, on_hi = (dh == 0) & (dl != 0), (dl == 0) & (dh != 0)
            charge = jnp.where(on_lo, 0, jnp.where(on_hi, 1, ic))
            i, j = (dl, dh) if ic == 0 else (dh, dl)
            at = 2 * k - 1 + (i - 1) * (k - 1) + j - 1
            at = jnp.where(on_lo, 2 * dl - 1 + (ic != 0), jnp.where(on_hi, 2 * dh - 1 + (ic != 1), at))
            at = jnp.where((dh == 0) & (dl == 0), 0, at)
            source = jnp.where(charge == c, 0, k * k) + at
        else:
            other, at = n // (k * k), n % (k * k)
            charge = c ^ other
            if at == 0:
                i, j, core = 0, 0, charge
            elif at < 2 * k - 1:
                i, j, core = (at + 1) // 2, 0, charge ^ ((at + 1) % 2)
            else:
                i, j, core = (at - 2 * k + 1) // (k - 1) + 1, (at - 2 * k + 1) % (k - 1) + 1, charge
            dh, dl = jnp.where(charge == 0, j, i), jnp.where(charge == 0, i, j)
            source = ((h - dh) % k * k + (l - dl) % k) * 2 + core
        picked.append(source)
    return jnp.stack(picked).astype(jnp.int32)


def exchange(value, axes):
    return lax.all_to_all(value, axes, split_axis=0, concat_axis=0, tiled=True)


def dot_rows(left, right):
    return lax.dot_general(left, right, (((1,), (1,)), ((), ())), preferred_element_type=F32)


def middle_kernel(
    share, wide, order_ref, hidden_ref, d_first_ref, d_second_ref, gate_ref, up_ref, inner_ref, d_gu_ref, keep_ref, give_ref
):
    hidden = hidden_ref[...]
    gate = jnp.dot(hidden, gate_ref[...], preferred_element_type=F32)
    up = jnp.dot(hidden, up_ref[...], preferred_element_type=F32)
    d_inner = jnp.concatenate([d_first_ref[0], d_second_ref[0]]).astype(F32)
    root = (2.0 / math.pi) ** 0.5
    square = gate * gate
    bent = jnp.tanh(root * gate * (1.0 + 0.044715 * square))
    half = 0.5 * (1.0 + bent)
    gelu = gate * half
    slope = half + 0.5 * gate * (1.0 - bent * bent) * (root * (1.0 + 3 * 0.044715 * square))
    d_gate = (d_inner * up * slope).astype(BF16)
    d_up = (d_inner * gelu).astype(BF16)
    inner_ref[:, :share] = (gelu * up).astype(BF16)
    d_gu_ref[:, :share] = d_gate
    d_gu_ref[:, wide : wide + share] = d_up
    if wide > share:
        rest = jnp.zeros((hidden.shape[0], wide - share), BF16)
        inner_ref[:, share:] = rest
        d_gu_ref[:, share:wide] = rest
        d_gu_ref[:, wide + share :] = rest
    back = (dot_rows(d_gate, gate_ref[...]) + dot_rows(d_up, up_ref[...])).astype(BF16)
    step, steps = pl.program_id(0), pl.num_programs(0)

    @pl.when(step < steps // 2)
    def _():
        keep_ref[...] = back

    @pl.when(step >= steps // 2)
    def _():
        give_ref[...] = back


def feed_forward(hidden, d_inner, order, w_gate, w_up, wide):
    length, width = hidden.shape
    block, share = d_inner.shape[1:]
    rows = 2 * block
    steps = length // rows
    weight = pl.BlockSpec((width, share), lambda n, order_ref: (0, 0), pipeline_mode=pl.Buffered(1))
    return pl.pallas_call(
        functools.partial(middle_kernel, share, wide),
        out_shape=(
            jax.ShapeDtypeStruct((length, wide), BF16),
            jax.ShapeDtypeStruct((length, 2 * wide), BF16),
            jax.ShapeDtypeStruct((length // 2, width), BF16),
            jax.ShapeDtypeStruct((length // 2, width), BF16),
        ),
        grid_spec=pltpu.PrefetchScalarGridSpec(
            num_scalar_prefetch=1,
            grid=(steps,),
            in_specs=[
                pl.BlockSpec((rows, width), lambda n, order_ref: (n, 0)),
                pl.BlockSpec((1, block, share), lambda n, order_ref: (order_ref[2 * n], 0, 0)),
                pl.BlockSpec((1, block, share), lambda n, order_ref: (order_ref[2 * n + 1], 0, 0)),
                weight,
                weight,
            ],
            out_specs=[
                pl.BlockSpec((rows, wide), lambda n, order_ref: (n, 0)),
                pl.BlockSpec((rows, 2 * wide), lambda n, order_ref: (n, 0)),
                pl.BlockSpec((rows, width), lambda n, order_ref: (jnp.minimum(n, steps // 2 - 1), 0)),
                pl.BlockSpec((rows, width), lambda n, order_ref: (jnp.maximum(n - steps // 2, 0), 0)),
            ],
        ),
        compiler_params=pltpu.CompilerParams(vmem_limit_bytes=48 * 2**20),
        cost_estimate=pl.CostEstimate(
            flops=8 * length * width * share,
            bytes_accessed=4 * length * width + 4 * width * share,
            transcendentals=length * share,
        ),
        name="feed_forward",
    )(order, hidden, d_inner, d_inner, w_gate, w_up)


def norm_scale(value):
    return lax.rsqrt(jnp.mean(value * value, axis=-1, keepdims=True) + EPS)


def norm_backward(d_normed, normed, scale):
    return scale * (d_normed - normed * jnp.mean(d_normed * normed, axis=-1, keepdims=True))


def with_gain(weight, gain):
    return (weight.astype(F32) * gain.astype(F32)[:, None]).astype(BF16)


def in_place(mine, other, at):
    both = jnp.zeros(mine.shape[:1] + (2,) + mine.shape[1:], mine.dtype)
    rest = (0,) * (mine.ndim - 1)
    both = lax.dynamic_update_slice(both, mine[:, None], (0, at) + rest)
    return lax.dynamic_update_slice(both, other[:, None], (0, 1 - at) + rest)


def per_device(
    tokens, cotangent, gain_attn, w_query, w_keyval, w_out, b_out, gain_ffn, w_gateup, w_down
):
    block_len, width = tokens.shape[1:]
    n_ctx = lax.axis_size("hi") * lax.axis_size("lo") * lax.axis_size("core")
    n_far, n_near = lax.axis_size("far"), lax.axis_size("near")
    n_seq = n_far * n_near
    n_all = n_ctx * n_seq
    n_group = n_ctx * n_far
    rows = w_query.shape[0]
    length = n_ctx * block_len
    q_scale = HD ** (-0.5)
    position = (lax.axis_index("hi") * lax.axis_size("lo") + lax.axis_index("lo")) * 2 + lax.axis_index("core")
    far, near = lax.axis_index("far"), lax.axis_index("near")
    q_cols = NH * HD // n_ctx
    kv_cols = 2 * HD // n_ctx
    share = FF // n_group
    quarter = width // n_seq

    block = tokens.reshape(block_len, width)
    d_final = cotangent.reshape(block_len, width)
    residual = block.astype(F32)

    qkv_send = jnp.concatenate(
        [
            with_gain(w_query, gain_attn).reshape(rows, n_ctx, q_cols),
            with_gain(w_keyval, gain_attn).reshape(rows, n_ctx, kv_cols),
        ],
        axis=2,
    ).transpose(1, 0, 2)
    qkv_send = jnp.broadcast_to(qkv_send[:, None], (n_ctx, n_seq) + qkv_send.shape[1:])
    scale1 = norm_scale(residual)
    normed1 = residual * scale1
    vectors = jnp.stack([gain_attn, b_out, gain_ffn])
    vectors = jnp.pad(vectors, ((0, 13), (0, width - rows)))
    out_send = jnp.concatenate([w_out, vectors])[None]
    out_near = send(out_send, "near", 1)
    down_other = send(w_down, "near", 1)
    out_far = send(out_send, "far", 1)
    out_both = lax.ppermute(out_send, SEQ, [(i, (i + n_near) % n_seq ^ 1) for i in range(n_seq)])
    hidden1 = lax.all_gather(normed1.astype(BF16), CTX, axis=0, tiled=True)
    w_qkv = exchange(qkv_send.reshape((n_all,) + qkv_send.shape[2:]), EVERY)
    gateup_send = with_gain(w_gateup, gain_ffn).reshape(rows, 2, n_group, share).transpose(1, 2, 0, 3)

    hidden1, w_qkv, gateup_send, out_near, out_far, out_both, d_start, down_other = meet(
        hidden1,
        w_qkv.reshape(width, q_cols + kv_cols),
        gateup_send,
        out_near,
        out_far,
        out_both,
        d_final,
        down_other,
    )
    gate_half = exchange(gateup_send[0], GROUP)
    f_theirs = send(d_start, "far", 1)

    def along_seq(part):
        mine = in_place(part(out_send), part(out_near), near)
        other = in_place(part(out_far), part(out_both), near)
        return in_place(mine, other, far)

    out_rows = along_seq(lambda value: value[:, :rows]).reshape(n_seq * rows, width)
    vectors = along_seq(lambda value: value[:, rows : rows + 3, :rows]).reshape(-1)
    full_out = lax.all_gather(out_rows, CTX, axis=0, tiled=True)

    qkv = dot(hidden1, w_qkv)
    qkv = jnp.concatenate([qkv[:, :q_cols] * q_scale, qkv[:, q_cols:]], axis=1).astype(BF16)
    qkv = qkv.reshape(n_ctx, block_len, q_cols + kv_cols)
    kv_send = qkv[:, :, q_cols:].transpose(1, 0, 2).reshape(block_len, 2 * HD)
    kv_send = jnp.broadcast_to(kv_send[None], (n_ctx, block_len, 2 * HD))
    spare = block_len * 8 - n_seq * 3 * rows
    extra = jnp.concatenate([vectors, jnp.zeros((spare,), BF16)]).reshape(1, block_len, 8)
    extra = jnp.broadcast_to(extra, (n_ctx, block_len, 8))
    q_send = jnp.concatenate([qkv[:, :, :q_cols], kv_send, extra], axis=2)
    q_send, gate_half = meet(q_send, gate_half)
    came = exchange(q_send, CTX)
    gate_other = send(gate_half, "near", 1)
    came, up_send = meet(came, gateup_send[1])
    cut = -(-rows * 3 // 5 // 16) * 16
    up_first = exchange(up_send[:, :cut], GROUP)
    vectors = came[:, :, q_cols + 2 * HD :].reshape(n_ctx, -1)[:, : n_seq * 3 * rows]
    vectors = vectors.reshape(n_ctx * n_seq, 3, rows).transpose(1, 0, 2).reshape(3, width).astype(F32)
    gain1, bias, gain2 = vectors[0], vectors[1], vectors[2]
    query = came[:, :, :q_cols].transpose(1, 0, 2).reshape(block_len, NH, HD)
    keyval = came[:, :, q_cols : q_cols + 2 * HD].reshape(n_ctx, block_len, n_ctx, kv_cols).transpose(2, 1, 0, 3)
    keyval = keyval.reshape(length, 2 * HD)
    key, value = keyval[:, :HD], keyval[:, HD:]
    spacing = (position * block_len + jnp.arange(block_len, dtype=jnp.int32))[:, None] - jnp.arange(
        length, dtype=jnp.int32
    )[None, :]
    allowed = (spacing >= 0) & (spacing < WINDOW)
    scores = jnp.einsum("qhd,kd->hqk", query, key, preferred_element_type=F32)
    scores = jnp.where(allowed[None], scores, NEG)
    maximum = jnp.max(scores, axis=-1, keepdims=True)
    log_total = maximum + jnp.log(jnp.sum(jnp.exp(scores - maximum), axis=-1, keepdims=True))
    probs_low = jnp.exp(scores - log_total).astype(BF16)
    mixed = jnp.einsum("hqk,kd->qhd", probs_low, value, preferred_element_type=F32).astype(BF16)
    mixed = mixed.reshape(block_len, NH * HD)

    mixed, f_theirs, full_out, gate_other, up_first, up_send = meet(
        mixed, f_theirs, full_out, gate_other, up_first, up_send
    )
    up_second = exchange(up_send[:, cut:], GROUP)
    near_first = send(up_first, "near", 1)
    final_rows = lax.all_gather(jnp.concatenate([d_start, f_theirs]), CTX, axis=0, tiled=True)
    middle = residual + dot(mixed, full_out) + bias

    scale2 = norm_scale(middle)
    normed2 = middle * scale2
    hidden2 = normed2.astype(BF16)
    hidden2, up_second = meet(hidden2, up_second)
    m_pair = gather_0(hidden2)
    theirs = send(hidden2, "far", 1)
    near_second = send(up_second, "near", 1)
    m_sides = gather_1(m_pair)
    w_dn = in_place(w_down[None], down_other[None], near).reshape(share, width)
    devices = order_ctx(False)
    w_gate = in_place(gate_half, gate_other, near).reshape(width, share)
    m_sides, theirs, near_first, w_dn, w_gate = meet(m_sides, theirs, near_first, w_dn, w_gate)
    m_corners = gather_2(m_sides)
    t_pair = gather_0(theirs)
    m_corners, t_pair, near_second = meet(m_corners, t_pair, near_second)
    d_inner = dot_last(final_rows, w_dn).astype(BF16).reshape(2 * n_ctx, block_len, share)
    m_halves = gather_3(m_pair, m_sides, m_corners)
    t_sides = gather_1(t_pair)
    up_half = jnp.concatenate([up_first, up_second], axis=1)
    up_other = jnp.concatenate([near_first, near_second], axis=1)
    w_up = in_place(up_half, up_other, near).reshape(width, share)
    m_halves, t_sides, w_up, d_inner = meet(m_halves, t_sides, w_up, d_inner)
    t_corners = gather_2(t_sides)
    hidden_m = gather_all(m_pair, m_halves)
    t_corners, hidden_m = meet(t_corners, hidden_m)
    t_halves = gather_3(t_pair, t_sides, t_corners)

    wide = -(-share // 128) * 128
    half = length // 2
    mixed_send = mixed.reshape(block_len, n_ctx, q_cols).transpose(1, 0, 2)
    mixed_send, t_halves = meet(mixed_send, t_halves)
    mixed_cols = exchange(mixed_send, CTX)
    inner_m, d_gu_m, m_keep, m_give = feed_forward(hidden_m, d_inner, 2 * devices, w_gate, w_up, wide)
    m_give, t_halves = meet(m_give, t_halves)
    m_came = send(m_give, "core", 1)
    hidden_t = gather_all(t_pair, t_halves)
    inner_t, d_gu_t, t_keep, t_give = feed_forward(hidden_t, d_inner, 2 * devices + 1, w_gate, w_up, wide)
    t_give, m_keep, m_came, mixed_cols, inner_m = meet(t_give, m_keep, m_came, mixed_cols, inner_m)
    t_came = send(t_give, "core", 1)
    m_back = scatter_1(m_keep, m_came, block_len)
    mixed_cols = pick_blocks(mixed_cols, devices).reshape(length, q_cols)
    places = order_ctx(True)
    inner_rows = jnp.concatenate([inner_m, inner_t]).reshape(2 * n_ctx, block_len, wide)
    inner_rows = pick_blocks(inner_rows, jnp.stack([places, places + n_ctx], axis=1).reshape(-1))
    mixed_cols, inner_rows, t_keep, t_came, m_back, m_keep, m_came, inner_m, inner_t = meet(
        mixed_cols, inner_rows, t_keep, t_came, m_back, m_keep, m_came, inner_m, inner_t
    )
    t_back = scatter_1(t_keep, t_came, block_len)
    m_sides = scatter_2(m_keep, m_came, m_back, block_len)
    out_give = dot(jnp.concatenate([inner_m[half:, :share], inner_t[half:, :share]]), w_dn).astype(BF16)
    out_keep = dot(jnp.concatenate([inner_m[:half, :share], inner_t[:half, :share]]), w_dn).astype(BF16)
    out_give, out_keep, t_back, t_keep, t_came, d_gu_m, d_gu_t = meet(
        out_give, out_keep, t_back, t_keep, t_came, d_gu_m, d_gu_t
    )
    t_sides = scatter_2(t_keep, t_came, t_back, block_len)

    gu_grad = dot_first(jnp.concatenate([hidden_m, hidden_t]), jnp.concatenate([d_gu_m, d_gu_t]))
    gu_grad, t_sides, m_sides, t_keep, t_came, inner_rows = meet(
        gu_grad.astype(BF16), t_sides, m_sides, t_keep, t_came, inner_rows
    )
    t_other = scatter_3(t_sides)
    m_other = scatter_3(m_sides)
    theirs = scatter_4(t_keep, t_came, t_sides, t_other, block_len).astype(BF16)
    theirs, inner_rows = meet(theirs, inner_rows)
    theirs = send(theirs, "far", 1)
    down_grad = dot_first(final_rows, inner_rows.reshape(2 * length, wide)).astype(BF16)
    ffn_grad = [value.reshape(n_far, n_near, quarter, -1) for value in (gu_grad, down_grad)]
    ffn_grad = jnp.stack(
        [jnp.concatenate([value[:, n] for value in ffn_grad], axis=2) for n in range(n_near)]
    )
    m_other, theirs = meet(m_other, theirs)
    ffn_grad = lax.psum_scatter(ffn_grad, "near", scatter_dimension=0, tiled=True)
    d_hidden2 = scatter_4(m_keep, m_came, m_sides, m_other, block_len) + theirs.astype(F32)

    d_middle = d_final.astype(F32) + norm_backward(d_hidden2, normed2, scale2)
    d_gain2 = jnp.sum(d_hidden2 * normed2, axis=0) / gain2
    d_bias = jnp.sum(d_middle, axis=0)
    d_low = d_middle.astype(BF16)
    d_low, out_give = meet(d_low, out_give)
    l_pair = gather_0(d_low)
    l_pair, d_low, out_give = meet(l_pair, d_low, out_give)
    l_sides = gather_1(l_pair)
    o_came = send(out_give, "core", 1)
    d_mixed = dot_last(d_low, full_out).astype(BF16)
    d_mixed, o_came = meet(d_mixed, o_came)
    o_back = scatter_1(out_keep, o_came, block_len)
    d_mixed = d_mixed.reshape(block_len, NH, HD)
    scores = jnp.einsum("qhd,kd->hqk", query, key, preferred_element_type=F32)
    scores = jnp.where(allowed[None], scores, NEG)
    probs = jnp.exp(scores - log_total)
    probs_again = probs.astype(BF16)
    d_probs = jnp.einsum("qhd,kd->hqk", d_mixed, value, preferred_element_type=F32)
    delta = jnp.sum(probs * d_probs, axis=-1, keepdims=True)
    d_scores = (probs * (d_probs - delta)).astype(BF16)
    d_query = jnp.einsum("hqk,kd->qhd", d_scores, key, preferred_element_type=F32) * q_scale
    d_key = jnp.einsum("hqk,qhd->kd", d_scores, query, preferred_element_type=F32)
    d_value = jnp.einsum("hqk,qhd->kd", probs_again, d_mixed, preferred_element_type=F32)
    d_query = d_query.reshape(block_len, n_ctx, q_cols).astype(BF16).transpose(1, 0, 2)
    d_keyval = jnp.concatenate([d_key, d_value], axis=1).astype(BF16)
    d_keyval = d_keyval.reshape(n_ctx, block_len, n_ctx, kv_cols).transpose(2, 1, 0, 3)
    d_keyval = d_keyval.reshape(n_ctx, block_len, 2 * HD)
    d_send = jnp.concatenate([d_query, d_keyval], axis=2)
    d_send, l_sides, o_back, out_keep, o_came = meet(d_send, l_sides, o_back, out_keep, o_came)
    came = exchange(d_send, CTX)
    l_corners = gather_2(l_sides)
    o_sides = scatter_2(out_keep, o_came, o_back, block_len)
    came, l_corners, ffn_grad = meet(came, l_corners, ffn_grad)
    ffn_grad = exchange(ffn_grad[0], ("far",))
    l_halves = gather_3(l_pair, l_sides, l_corners)
    d_keyval = jnp.sum(came[:, :, q_cols:].astype(F32), axis=0).astype(BF16)
    d_keyval = d_keyval.reshape(block_len, n_ctx, kv_cols).transpose(1, 0, 2)
    d_qkv = jnp.concatenate([came[:, :, :q_cols], d_keyval], axis=2)
    d_back = pick_blocks(d_qkv, devices).reshape(length, q_cols + kv_cols)
    d_qkv = d_qkv.reshape(length, q_cols + kv_cols)
    e_came = send(dot_last(d_back[half:], w_qkv).astype(BF16), "core", 1)
    e_keep = dot_last(d_back[:half], w_qkv).astype(BF16)
    e_keep, e_came, l_halves, o_sides, d_qkv = meet(e_keep, e_came, l_halves, o_sides, d_qkv)
    e_back = scatter_1(e_keep, e_came, block_len)
    o_other = scatter_3(o_sides)
    out_grad = dot_first(gather_all(l_pair, l_halves), mixed_cols)
    qkv_grad = dot_first(hidden1, d_qkv)
    d_gain1 = jnp.sum(qkv_grad * w_qkv.astype(F32), axis=1) / gain1
    attn_grad = jnp.concatenate([qkv_grad.astype(BF16), out_grad.astype(BF16)], axis=1)
    e_back, o_other, out_keep, o_came = meet(e_back, o_other, out_keep, o_came)
    e_sides = scatter_2(e_keep, e_came, e_back, block_len)
    sums = jnp.stack([d_gain1, d_bias, d_gain2]).reshape(3, n_all, rows).transpose(1, 0, 2)
    e_sides, attn_grad, sums, ffn_grad = meet(e_sides, attn_grad, sums, ffn_grad)
    attn_grad = lax.psum_scatter(attn_grad, SEQ, scatter_dimension=0, tiled=True)
    e_other = scatter_3(e_sides)
    o_total = scatter_4(out_keep, o_came, o_sides, o_other, block_len)
    o_theirs = send(o_total[block_len:].astype(BF16), "far", 1)
    d_normed1 = scatter_4(e_keep, e_came, e_sides, e_other, block_len)
    d_input = d_middle + norm_backward(d_normed1, normed1, scale1)
    output = (middle + o_total[:block_len] + o_theirs.astype(F32)).astype(BF16)
    count = n_ctx // 2
    odd = position % 2
    gate, up = ffn_grad[:, :, :wide], ffn_grad[:, :, wide : 2 * wide]
    pieces = []
    for flip in range(2):
        pairs = [(c, ((c % 2) ^ flip) * count + c // 2) for c in range(n_ctx)]
        pieces.append(lax.ppermute(jnp.where(odd == flip, gate, up), CTX, pairs))
    down_grad = ffn_grad[:, :, 2 * wide : 2 * wide + share].transpose(0, 2, 1)
    down_grad = down_grad.reshape(n_far * share, quarter).astype(F32)
    upper = position >= count
    columns = [jnp.where(upper, pieces[1], pieces[0]), jnp.where(upper, pieces[0], pieces[1])]
    own_gain = lax.dynamic_slice_in_dim(gain2, (far * n_near + near) * quarter, quarter)
    gateup_grad = (
        jnp.concatenate([columns[i][f][:, :share] for i in range(2) for f in range(n_far)], axis=1).astype(F32)
        * own_gain[:, None]
    )
    sums, d_input, down_grad = meet(sums, d_input, down_grad)
    sums = exchange(sums, EVERY)
    sums, attn_grad, output, gateup_grad = meet(sums, attn_grad, output, gateup_grad)
    sums = jnp.sum(sums, axis=0)
    attn_grad = attn_grad.astype(F32)
    own_gain = lax.dynamic_slice_in_dim(gain1, (far * n_near + near) * quarter, quarter)
    qkv_grad = attn_grad[:, : q_cols + kv_cols] * own_gain[:, None]
    out_grad = attn_grad[:, q_cols + kv_cols :].T
    return (
        output.reshape(1, block_len, width),
        d_input.reshape(1, block_len, width),
        sums[0],
        qkv_grad[:, :q_cols],
        qkv_grad[:, q_cols:],
        out_grad,
        sums[1],
        sums[2],
        gateup_grad,
        down_grad,
    )


def solution(mesh):
    n_ctx, n_seq = mesh.shape["ctx"], mesh.shape["seq"]
    side = math.isqrt(n_ctx // 2)
    fine = Mesh(
        mesh.devices.reshape(n_ctx // 2 // side, side, 2, n_seq // 2, 2), EVERY
    )
    whole = P(EVERY)
    return jax.shard_map(
        per_device,
        mesh=fine,
        in_specs=(
            P(SEQ, CTX, None),
            P(SEQ, CTX, None),
            whole,
            whole,
            whole,
            whole,
            whole,
            whole,
            whole,
            whole,
        ),
        out_specs=(
            P(SEQ, CTX, None),
            P(SEQ, CTX, None),
            whole,
            P(SEQ, CTX),
            P(SEQ, CTX),
            P(CTX, SEQ),
            whole,
            whole,
            P(SEQ, CTX),
            P(CTX, SEQ),
        ),
        check_vma=False,
    )
```

```python
import functools
import math

import jax
import jax.numpy as jnp
from jax import lax
from jax.experimental import pallas as pl
from jax.experimental.pallas import tpu as pltpu
from jax.sharding import Mesh, PartitionSpec as P

NH = 10
HD = 256
FF = 7680
WINDOW = 2048

EPS = 1e-06
NEG = -1e30

F32 = jnp.float32
BF16 = jnp.bfloat16

CTX = ("hi", "lo", "core")
GROUP = ("hi", "lo", "core", "far")
SEQ = ("far", "near")
EVERY = ("hi", "lo", "core", "far", "near")


def dot(left, right):
    return jnp.dot(left, right, preferred_element_type=F32)


def dot_last(left, right):
    return lax.dot_general(left, right, (((1,), (1,)), ((), ())), preferred_element_type=F32)


def dot_first(left, right):
    return lax.dot_general(left, right, (((0,), (0,)), ((), ())), preferred_element_type=F32)


def send(value, axis, step):
    count = lax.axis_size(axis)
    return lax.ppermute(value, axis, [(i, (i + step) % count) for i in range(count)])


def meet(*values):
    return lax.optimization_barrier(values)


def side():
    return lax.axis_size("lo")


def send_cross(value, step, second):
    k = side()
    pairs = []
    for h in range(k):
        for l in range(k):
            for c in range(2):
                along_lo = (c == 0) != second
                to_h, to_l = (h, (l + step) % k) if along_lo else ((h + step) % k, l)
                pairs.append(((h * k + l) * 2 + c, (to_h * k + to_l) * 2 + c))
    return lax.ppermute(value, CTX, pairs)


def gather_0(block):
    return jnp.concatenate([block, send(block, "core", 1)])


def gather_1(pair):
    return [send_cross(pair, i, False) for i in range(1, side())]


def gather_2(sides):
    rows = sides[0].shape[0] // 2
    return [send_cross(value[:rows], j, True) for value in sides for j in range(1, side())]


def gather_3(pair, sides, corners):
    own = jnp.concatenate(sides + corners)
    return own, send(own, "core", 1)


def gather_all(pair, halves):
    rows = pair.shape[0] // 2
    return jnp.concatenate([pair[:rows], halves[0], pair[rows:], halves[1]])


def add(*values):
    return sum((value.astype(F32) for value in values[1:]), values[0].astype(F32))


def block_of(value, at, rows):
    k = side()
    value = value.reshape(-1, k * k, rows, value.shape[-1])[:, at]
    return value.reshape(-1, value.shape[-1])


def scatter_1(keep, came, rows):
    k = side()
    back = []
    for i in range(k - 1):
        for j in range(1, k):
            at = 2 * k - 1 + i * (k - 1) + j - 1
            low = add(block_of(keep, at, rows), block_of(came, at, rows)).astype(BF16)
            back.append(send_cross(low, -j, True))
    return back


def scatter_2(keep, came, back, rows):
    k = side()
    sides = []
    for i in range(1, k):
        first = add(block_of(keep, 2 * i - 1, rows), block_of(came, 2 * i - 1, rows))
        first = add(first, *back[(i - 1) * (k - 1) : i * (k - 1)])
        second = add(block_of(keep, 2 * i, rows), block_of(came, 2 * i, rows))
        sides.append(send_cross(jnp.concatenate([first, second]).astype(BF16), -i, False))
    return sides


def scatter_3(sides):
    half = sides[0].shape[0] // 2
    return send(add(*[value[half:] for value in sides]).astype(BF16), "core", 1)


def scatter_4(keep, came, sides, other, rows):
    half = sides[0].shape[0] // 2
    return add(
        block_of(keep, 0, rows), block_of(came, 0, rows), other, *[value[:half] for value in sides]
    )


def copy_blocks(order_ref, from_ref, to_ref):
    for n in range(to_ref.shape[0]):
        to_ref[n] = from_ref[order_ref[n]]


def pick_blocks(blocks, order):
    shape = order.shape + blocks.shape[1:]
    return pl.pallas_call(
        copy_blocks,
        out_shape=jax.ShapeDtypeStruct(shape, blocks.dtype),
        in_specs=[pl.BlockSpec(memory_space=pltpu.SMEM), pl.BlockSpec(memory_space=pltpu.VMEM)],
        out_specs=pl.BlockSpec(memory_space=pltpu.VMEM),
        cost_estimate=pl.CostEstimate(
            flops=0, bytes_accessed=2 * blocks.size * blocks.dtype.itemsize, transcendentals=0
        ),
        name="pick_blocks",
    )(order, blocks)


def order_ctx(by_device):
    k = side()
    h, l, c = (lax.axis_index(axis) for axis in CTX)
    picked = []
    for n in range(2 * k * k):
        if by_device:
            ih, il, ic = n // (2 * k), n // 2 % k, n % 2
            dh, dl = (h - ih) % k, (l - il) % k
            on_lo, on_hi = (dh == 0) & (dl != 0), (dl == 0) & (dh != 0)
            charge = jnp.where(on_lo, 0, jnp.where(on_hi, 1, ic))
            i, j = (dl, dh) if ic == 0 else (dh, dl)
            at = 2 * k - 1 + (i - 1) * (k - 1) + j - 1
            at = jnp.where(on_lo, 2 * dl - 1 + (ic != 0), jnp.where(on_hi, 2 * dh - 1 + (ic != 1), at))
            at = jnp.where((dh == 0) & (dl == 0), 0, at)
            source = jnp.where(charge == c, 0, k * k) + at
        else:
            other, at = n // (k * k), n % (k * k)
            charge = c ^ other
            if at == 0:
                i, j, core = 0, 0, charge
            elif at < 2 * k - 1:
                i, j, core = (at + 1) // 2, 0, charge ^ ((at + 1) % 2)
            else:
                i, j, core = (at - 2 * k + 1) // (k - 1) + 1, (at - 2 * k + 1) % (k - 1) + 1, charge
            dh, dl = jnp.where(charge == 0, j, i), jnp.where(charge == 0, i, j)
            source = ((h - dh) % k * k + (l - dl) % k) * 2 + core
        picked.append(source)
    return jnp.stack(picked).astype(jnp.int32)


def exchange(value, axes):
    return lax.all_to_all(value, axes, split_axis=0, concat_axis=0, tiled=True)


def dot_rows(left, right):
    return lax.dot_general(left, right, (((1,), (1,)), ((), ())), preferred_element_type=F32)


def middle_kernel(
    share, wide, order_ref, hidden_ref, d_first_ref, d_second_ref, gate_ref, up_ref, inner_ref, d_gu_ref, keep_ref, give_ref
):
    hidden = hidden_ref[...]
    gate = jnp.dot(hidden, gate_ref[...], preferred_element_type=F32)
    up = jnp.dot(hidden, up_ref[...], preferred_element_type=F32)
    d_inner = jnp.concatenate([d_first_ref[0], d_second_ref[0]]).astype(F32)
    root = (2.0 / math.pi) ** 0.5
    square = gate * gate
    bent = jnp.tanh(root * gate * (1.0 + 0.044715 * square))
    half = 0.5 * (1.0 + bent)
    gelu = gate * half
    slope = half + 0.5 * gate * (1.0 - bent * bent) * (root * (1.0 + 3 * 0.044715 * square))
    d_gate = (d_inner * up * slope).astype(BF16)
    d_up = (d_inner * gelu).astype(BF16)
    inner_ref[:, :share] = (gelu * up).astype(BF16)
    d_gu_ref[:, :share] = d_gate
    d_gu_ref[:, wide : wide + share] = d_up
    if wide > share:
        rest = jnp.zeros((hidden.shape[0], wide - share), BF16)
        inner_ref[:, share:] = rest
        d_gu_ref[:, share:wide] = rest
        d_gu_ref[:, wide + share :] = rest
    back = (dot_rows(d_gate, gate_ref[...]) + dot_rows(d_up, up_ref[...])).astype(BF16)
    step, steps = pl.program_id(0), pl.num_programs(0)

    @pl.when(step < steps // 2)
    def _():
        keep_ref[...] = back

    @pl.when(step >= steps // 2)
    def _():
        give_ref[...] = back


def feed_forward(hidden, d_inner, order, w_gate, w_up, wide):
    length, width = hidden.shape
    block, share = d_inner.shape[1:]
    rows = 2 * block
    steps = length // rows
    weight = pl.BlockSpec((width, share), lambda n, order_ref: (0, 0), pipeline_mode=pl.Buffered(1))
    return pl.pallas_call(
        functools.partial(middle_kernel, share, wide),
        out_shape=(
            jax.ShapeDtypeStruct((length, wide), BF16),
            jax.ShapeDtypeStruct((length, 2 * wide), BF16),
            jax.ShapeDtypeStruct((length // 2, width), BF16),
            jax.ShapeDtypeStruct((length // 2, width), BF16),
        ),
        grid_spec=pltpu.PrefetchScalarGridSpec(
            num_scalar_prefetch=1,
            grid=(steps,),
            in_specs=[
                pl.BlockSpec((rows, width), lambda n, order_ref: (n, 0)),
                pl.BlockSpec((1, block, share), lambda n, order_ref: (order_ref[2 * n], 0, 0)),
                pl.BlockSpec((1, block, share), lambda n, order_ref: (order_ref[2 * n + 1], 0, 0)),
                weight,
                weight,
            ],
            out_specs=[
                pl.BlockSpec((rows, wide), lambda n, order_ref: (n, 0)),
                pl.BlockSpec((rows, 2 * wide), lambda n, order_ref: (n, 0)),
                pl.BlockSpec((rows, width), lambda n, order_ref: (jnp.minimum(n, steps // 2 - 1), 0)),
                pl.BlockSpec((rows, width), lambda n, order_ref: (jnp.maximum(n - steps // 2, 0), 0)),
            ],
        ),
        compiler_params=pltpu.CompilerParams(vmem_limit_bytes=48 * 2**20),
        cost_estimate=pl.CostEstimate(
            flops=8 * length * width * share,
            bytes_accessed=4 * length * width + 4 * width * share,
            transcendentals=length * share,
        ),
        name="feed_forward",
    )(order, hidden, d_inner, d_inner, w_gate, w_up)


def gradient_kernel(both, hidden_ref, more_ref, final_ref, d_gu_ref, d_more_ref, inner_ref, grad_ref):
    grad_ref[0, 0, :, :both] = (
        dot_first(hidden_ref[...], d_gu_ref[...]) + dot_first(more_ref[...], d_more_ref[...])
    ).astype(BF16)
    grad_ref[0, 0, :, both:] = dot_first(final_ref[...], inner_ref[...]).astype(BF16)


def weight_gradients(hidden, d_gu, final, inner, n_far, n_near):
    length, width = hidden[0].shape
    quarter = width // (n_far * n_near)
    both, wide = d_gu[0].shape[1], inner.shape[1]
    rows = quarter if 16 * length * quarter <= 2**24 else 128
    steps = quarter // rows

    def columns(n, f, k):
        return (0, (f * n_near + n) * steps + k)

    def whole(value):
        return pl.BlockSpec(value.shape, lambda n, f, k: (0, 0), pipeline_mode=pl.Buffered(1))

    return pl.pallas_call(
        functools.partial(gradient_kernel, both),
        out_shape=jax.ShapeDtypeStruct((n_near, n_far, quarter, both + wide), BF16),
        grid=(n_near, n_far, steps),
        in_specs=[
            pl.BlockSpec((length, rows), columns),
            pl.BlockSpec((length, rows), columns),
            pl.BlockSpec((final.shape[0], rows), columns),
            whole(d_gu[0]),
            whole(d_gu[1]),
            whole(inner),
        ],
        out_specs=pl.BlockSpec((1, 1, rows, both + wide), lambda n, f, k: (n, f, k, 0)),
        compiler_params=pltpu.CompilerParams(vmem_limit_bytes=48 * 2**20),
        cost_estimate=pl.CostEstimate(
            flops=4 * length * width * (both + wide),
            bytes_accessed=8 * length * width + 2 * width * (both + wide),
            transcendentals=0,
        ),
        name="weight_gradients",
    )(*hidden, final, *d_gu, inner)


def two_gradients_kernel(left_ref, d_left_ref, right_ref, d_right_ref, grad_ref):
    split = d_left_ref.shape[1]
    grad_ref[:, :split] = dot_first(left_ref[...], d_left_ref[...]).astype(BF16)
    grad_ref[:, split:] = dot_first(right_ref[...], d_right_ref[...]).astype(BF16)


def two_gradients(left, d_left, right, d_right):
    length, width = left.shape
    rows = 256 if length <= 1024 else 128
    total = d_left.shape[1] + d_right.shape[1]

    def whole(value):
        return pl.BlockSpec(value.shape, lambda n: (0, 0), pipeline_mode=pl.Buffered(1))

    return pl.pallas_call(
        two_gradients_kernel,
        out_shape=jax.ShapeDtypeStruct((width, total), BF16),
        grid=(width // rows,),
        in_specs=[
            pl.BlockSpec((length, rows), lambda n: (0, n)),
            whole(d_left),
            pl.BlockSpec((length, rows), lambda n: (0, n)),
            whole(d_right),
        ],
        out_specs=pl.BlockSpec((rows, total), lambda n: (n, 0)),
        compiler_params=pltpu.CompilerParams(vmem_limit_bytes=32 * 2**20),
        cost_estimate=pl.CostEstimate(
            flops=2 * length * width * total,
            bytes_accessed=4 * length * width + 2 * width * total,
            transcendentals=0,
        ),
        name="two_gradients",
    )(left, d_left, right, d_right)


def norm_scale(value):
    return lax.rsqrt(jnp.mean(value * value, axis=-1, keepdims=True) + EPS)


def norm_backward(d_normed, normed, scale):
    return scale * (d_normed - normed * jnp.mean(d_normed * normed, axis=-1, keepdims=True))


def with_gain(weight, gain):
    return (weight.astype(F32) * gain.astype(F32)[:, None]).astype(BF16)


def in_place(mine, other, at):
    both = jnp.zeros(mine.shape[:1] + (2,) + mine.shape[1:], mine.dtype)
    rest = (0,) * (mine.ndim - 1)
    both = lax.dynamic_update_slice(both, mine[:, None], (0, at) + rest)
    return lax.dynamic_update_slice(both, other[:, None], (0, 1 - at) + rest)


def per_device(
    tokens, cotangent, gain_attn, w_query, w_keyval, w_out, b_out, gain_ffn, w_gateup, w_down
):
    block_len, width = tokens.shape[1:]
    n_ctx = lax.axis_size("hi") * lax.axis_size("lo") * lax.axis_size("core")
    n_far, n_near = lax.axis_size("far"), lax.axis_size("near")
    n_seq = n_far * n_near
    n_all = n_ctx * n_seq
    n_group = n_ctx * n_far
    rows = w_query.shape[0]
    length = n_ctx * block_len
    q_scale = HD ** (-0.5)
    position = (lax.axis_index("hi") * lax.axis_size("lo") + lax.axis_index("lo")) * 2 + lax.axis_index("core")
    far, near = lax.axis_index("far"), lax.axis_index("near")
    q_cols = NH * HD // n_ctx
    kv_cols = 2 * HD // n_ctx
    share = FF // n_group
    quarter = width // n_seq

    block = tokens.reshape(block_len, width)
    d_final = cotangent.reshape(block_len, width)
    residual = block.astype(F32)

    qkv_send = jnp.concatenate(
        [
            with_gain(w_query, gain_attn).reshape(rows, n_ctx, q_cols),
            with_gain(w_keyval, gain_attn).reshape(rows, n_ctx, kv_cols),
        ],
        axis=2,
    ).transpose(1, 0, 2)
    qkv_send = jnp.broadcast_to(qkv_send[:, None], (n_ctx, n_seq) + qkv_send.shape[1:])
    scale1 = norm_scale(residual)
    normed1 = residual * scale1
    vectors = jnp.stack([gain_attn, b_out, gain_ffn])
    vectors = jnp.pad(vectors, ((0, 13), (0, width - rows)))
    out_send = jnp.concatenate([w_out, vectors])[None]
    out_near = send(out_send, "near", 1)
    down_other = send(w_down, "near", 1)
    out_far = send(out_send, "far", 1)
    out_both = lax.ppermute(out_send, SEQ, [(i, (i + n_near) % n_seq ^ 1) for i in range(n_seq)])
    hidden1 = lax.all_gather(normed1.astype(BF16), CTX, axis=0, tiled=True)
    w_qkv = exchange(qkv_send.reshape((n_all,) + qkv_send.shape[2:]), EVERY)
    gateup_send = with_gain(w_gateup, gain_ffn).reshape(rows, 2, n_group, share).transpose(1, 2, 0, 3)

    hidden1, w_qkv, gateup_send, out_near, out_far, out_both, d_start, down_other = meet(
        hidden1,
        w_qkv.reshape(width, q_cols + kv_cols),
        gateup_send,
        out_near,
        out_far,
        out_both,
        d_final,
        down_other,
    )
    gate_half = exchange(gateup_send[0], GROUP)
    f_theirs = send(d_start, "far", 1)

    def along_seq(part):
        mine = in_place(part(out_send), part(out_near), near)
        other = in_place(part(out_far), part(out_both), near)
        return in_place(mine, other, far)

    out_rows = along_seq(lambda value: value[:, :rows]).reshape(n_seq * rows, width)
    vectors = along_seq(lambda value: value[:, rows : rows + 3, :rows]).reshape(-1)
    full_out = lax.all_gather(out_rows, CTX, axis=0, tiled=True)

    qkv = dot(hidden1, w_qkv)
    qkv = jnp.concatenate([qkv[:, :q_cols] * q_scale, qkv[:, q_cols:]], axis=1).astype(BF16)
    qkv = qkv.reshape(n_ctx, block_len, q_cols + kv_cols)
    kv_send = qkv[:, :, q_cols:].transpose(1, 0, 2).reshape(block_len, 2 * HD)
    kv_send = jnp.broadcast_to(kv_send[None], (n_ctx, block_len, 2 * HD))
    spare = block_len * 8 - n_seq * 3 * rows
    extra = jnp.concatenate([vectors, jnp.zeros((spare,), BF16)]).reshape(1, block_len, 8)
    extra = jnp.broadcast_to(extra, (n_ctx, block_len, 8))
    q_send = jnp.concatenate([qkv[:, :, :q_cols], kv_send, extra], axis=2)
    q_send, gate_half = meet(q_send, gate_half)
    came = exchange(q_send, CTX)
    gate_other = send(gate_half, "near", 1)
    came, up_send = meet(came, gateup_send[1])
    cut = -(-rows * 3 // 5 // 16) * 16
    up_first = exchange(up_send[:, :cut], GROUP)
    vectors = came[:, :, q_cols + 2 * HD :].reshape(n_ctx, -1)[:, : n_seq * 3 * rows]
    vectors = vectors.reshape(n_ctx * n_seq, 3, rows).transpose(1, 0, 2).reshape(3, width).astype(F32)
    gain1, bias, gain2 = vectors[0], vectors[1], vectors[2]
    query = came[:, :, :q_cols].transpose(1, 0, 2).reshape(block_len, NH, HD)
    keyval = came[:, :, q_cols : q_cols + 2 * HD].reshape(n_ctx, block_len, n_ctx, kv_cols).transpose(2, 1, 0, 3)
    keyval = keyval.reshape(length, 2 * HD)
    key, value = keyval[:, :HD], keyval[:, HD:]
    spacing = (position * block_len + jnp.arange(block_len, dtype=jnp.int32))[:, None] - jnp.arange(
        length, dtype=jnp.int32
    )[None, :]
    allowed = (spacing >= 0) & (spacing < WINDOW)
    scores = jnp.einsum("qhd,kd->hqk", query, key, preferred_element_type=F32)
    scores = jnp.where(allowed[None], scores, NEG)
    maximum = jnp.max(scores, axis=-1, keepdims=True)
    log_total = maximum + jnp.log(jnp.sum(jnp.exp(scores - maximum), axis=-1, keepdims=True))
    probs_low = jnp.exp(scores - log_total).astype(BF16)
    mixed = jnp.einsum("hqk,kd->qhd", probs_low, value, preferred_element_type=F32).astype(BF16)
    mixed = mixed.reshape(block_len, NH * HD)

    mixed, f_theirs, full_out, gate_other, up_first, up_send = meet(
        mixed, f_theirs, full_out, gate_other, up_first, up_send
    )
    up_second = exchange(up_send[:, cut:], GROUP)
    near_first = send(up_first, "near", 1)
    final_rows = lax.all_gather(jnp.concatenate([d_start, f_theirs]), CTX, axis=0, tiled=True)
    middle = residual + dot(mixed, full_out) + bias

    scale2 = norm_scale(middle)
    normed2 = middle * scale2
    hidden2 = normed2.astype(BF16)
    hidden2, up_second = meet(hidden2, up_second)
    m_pair = gather_0(hidden2)
    theirs = send(hidden2, "far", 1)
    near_second = send(up_second, "near", 1)
    m_sides = gather_1(m_pair)
    w_dn = in_place(w_down[None], down_other[None], near).reshape(share, width)
    devices = order_ctx(False)
    w_gate = in_place(gate_half, gate_other, near).reshape(width, share)
    m_sides, theirs, near_first, w_dn, w_gate = meet(m_sides, theirs, near_first, w_dn, w_gate)
    m_corners = gather_2(m_sides)
    t_pair = gather_0(theirs)
    m_corners, t_pair, near_second = meet(m_corners, t_pair, near_second)
    d_inner = dot_last(final_rows, w_dn).astype(BF16).reshape(2 * n_ctx, block_len, share)
    m_halves = gather_3(m_pair, m_sides, m_corners)
    t_sides = gather_1(t_pair)
    up_half = jnp.concatenate([up_first, up_second], axis=1)
    up_other = jnp.concatenate([near_first, near_second], axis=1)
    w_up = in_place(up_half, up_other, near).reshape(width, share)
    m_halves, t_sides, w_up, d_inner = meet(m_halves, t_sides, w_up, d_inner)
    t_corners = gather_2(t_sides)
    hidden_m = gather_all(m_pair, m_halves)
    t_corners, hidden_m = meet(t_corners, hidden_m)
    t_halves = gather_3(t_pair, t_sides, t_corners)

    wide = -(-share // 128) * 128
    half = length // 2
    mixed_send = mixed.reshape(block_len, n_ctx, q_cols).transpose(1, 0, 2)
    mixed_send, t_halves = meet(mixed_send, t_halves)
    mixed_cols = exchange(mixed_send, CTX)
    inner_m, d_gu_m, m_keep, m_give = feed_forward(hidden_m, d_inner, 2 * devices, w_gate, w_up, wide)
    m_give, t_halves = meet(m_give, t_halves)
    m_came = send(m_give, "core", 1)
    hidden_t = gather_all(t_pair, t_halves)
    inner_t, d_gu_t, t_keep, t_give = feed_forward(hidden_t, d_inner, 2 * devices + 1, w_gate, w_up, wide)
    t_give, m_keep, m_came, mixed_cols, inner_m = meet(t_give, m_keep, m_came, mixed_cols, inner_m)
    t_came = send(t_give, "core", 1)
    m_back = scatter_1(m_keep, m_came, block_len)
    mixed_cols = pick_blocks(mixed_cols, devices).reshape(length, q_cols)
    places = order_ctx(True)
    inner_rows = jnp.concatenate([inner_m, inner_t]).reshape(2 * n_ctx, block_len, wide)
    inner_rows = pick_blocks(inner_rows, jnp.stack([places, places + n_ctx], axis=1).reshape(-1))
    mixed_cols, inner_rows, t_keep, t_came, m_back, m_keep, m_came, inner_m, inner_t = meet(
        mixed_cols, inner_rows, t_keep, t_came, m_back, m_keep, m_came, inner_m, inner_t
    )
    t_back = scatter_1(t_keep, t_came, block_len)
    m_sides = scatter_2(m_keep, m_came, m_back, block_len)
    out_give = dot(jnp.concatenate([inner_m[half:, :share], inner_t[half:, :share]]), w_dn).astype(BF16)
    out_keep = dot(jnp.concatenate([inner_m[:half, :share], inner_t[:half, :share]]), w_dn).astype(BF16)
    out_give, out_keep, t_back, t_keep, t_came, d_gu_m, d_gu_t = meet(
        out_give, out_keep, t_back, t_keep, t_came, d_gu_m, d_gu_t
    )
    t_sides = scatter_2(t_keep, t_came, t_back, block_len)

    ffn_grad = weight_gradients(
        (hidden_m, hidden_t),
        (d_gu_m, d_gu_t),
        final_rows,
        inner_rows.reshape(2 * length, wide),
        n_far,
        n_near,
    )
    ffn_grad, t_sides, m_sides, t_keep, t_came = meet(ffn_grad, t_sides, m_sides, t_keep, t_came)
    t_other = scatter_3(t_sides)
    m_other = scatter_3(m_sides)
    theirs = scatter_4(t_keep, t_came, t_sides, t_other, block_len).astype(BF16)
    theirs = send(theirs, "far", 1)
    m_other, theirs = meet(m_other, theirs)
    ffn_grad = lax.psum_scatter(ffn_grad, "near", scatter_dimension=0, tiled=True)
    d_hidden2 = scatter_4(m_keep, m_came, m_sides, m_other, block_len) + theirs.astype(F32)

    d_middle = d_final.astype(F32) + norm_backward(d_hidden2, normed2, scale2)
    d_gain2 = jnp.sum(d_hidden2 * normed2, axis=0) / gain2
    d_bias = jnp.sum(d_middle, axis=0)
    d_low = d_middle.astype(BF16)
    d_low, out_give = meet(d_low, out_give)
    l_pair = gather_0(d_low)
    l_pair, d_low, out_give = meet(l_pair, d_low, out_give)
    l_sides = gather_1(l_pair)
    o_came = send(out_give, "core", 1)
    d_mixed = dot_last(d_low, full_out).astype(BF16)
    d_mixed, o_came = meet(d_mixed, o_came)
    o_back = scatter_1(out_keep, o_came, block_len)
    d_mixed = d_mixed.reshape(block_len, NH, HD)
    scores = jnp.einsum("qhd,kd->hqk", query, key, preferred_element_type=F32)
    scores = jnp.where(allowed[None], scores, NEG)
    probs = jnp.exp(scores - log_total)
    probs_again = probs.astype(BF16)
    d_probs = jnp.einsum("qhd,kd->hqk", d_mixed, value, preferred_element_type=F32)
    delta = jnp.sum(probs * d_probs, axis=-1, keepdims=True)
    d_scores = (probs * (d_probs - delta)).astype(BF16)
    d_query = jnp.einsum("hqk,kd->qhd", d_scores, key, preferred_element_type=F32) * q_scale
    d_key = jnp.einsum("hqk,qhd->kd", d_scores, query, preferred_element_type=F32)
    d_value = jnp.einsum("hqk,qhd->kd", probs_again, d_mixed, preferred_element_type=F32)
    d_query = d_query.reshape(block_len, n_ctx, q_cols).astype(BF16).transpose(1, 0, 2)
    d_keyval = jnp.concatenate([d_key, d_value], axis=1).astype(BF16)
    d_keyval = d_keyval.reshape(n_ctx, block_len, n_ctx, kv_cols).transpose(2, 1, 0, 3)
    d_keyval = d_keyval.reshape(n_ctx, block_len, 2 * HD)
    d_send = jnp.concatenate([d_query, d_keyval], axis=2)
    d_send, l_sides, o_back, out_keep, o_came = meet(d_send, l_sides, o_back, out_keep, o_came)
    came = exchange(d_send, CTX)
    l_corners = gather_2(l_sides)
    o_sides = scatter_2(out_keep, o_came, o_back, block_len)
    came, l_corners, ffn_grad = meet(came, l_corners, ffn_grad)
    ffn_grad = exchange(ffn_grad[0], ("far",))
    l_halves = gather_3(l_pair, l_sides, l_corners)
    d_keyval = jnp.sum(came[:, :, q_cols:].astype(F32), axis=0).astype(BF16)
    d_keyval = d_keyval.reshape(block_len, n_ctx, kv_cols).transpose(1, 0, 2)
    d_qkv = jnp.concatenate([came[:, :, :q_cols], d_keyval], axis=2)
    d_back = pick_blocks(d_qkv, devices).reshape(length, q_cols + kv_cols)
    d_qkv = d_qkv.reshape(length, q_cols + kv_cols)
    e_came = send(dot_last(d_back[half:], w_qkv).astype(BF16), "core", 1)
    e_keep = dot_last(d_back[:half], w_qkv).astype(BF16)
    e_keep, e_came, l_halves, o_sides, d_qkv = meet(e_keep, e_came, l_halves, o_sides, d_qkv)
    e_back = scatter_1(e_keep, e_came, block_len)
    o_other = scatter_3(o_sides)
    attn_grad = two_gradients(hidden1, d_qkv, gather_all(l_pair, l_halves), mixed_cols)
    d_gain1 = attn_grad[:, : q_cols + kv_cols].astype(F32) * w_qkv.astype(F32)
    d_gain1 = jnp.sum(d_gain1, axis=1) / gain1
    e_back, o_other, out_keep, o_came = meet(e_back, o_other, out_keep, o_came)
    e_sides = scatter_2(e_keep, e_came, e_back, block_len)
    sums = jnp.stack([d_gain1, d_bias, d_gain2]).reshape(3, n_all, rows).transpose(1, 0, 2)
    e_sides, attn_grad, sums, ffn_grad = meet(e_sides, attn_grad, sums, ffn_grad)
    attn_grad = lax.psum_scatter(attn_grad, SEQ, scatter_dimension=0, tiled=True)
    e_other = scatter_3(e_sides)
    o_total = scatter_4(out_keep, o_came, o_sides, o_other, block_len)
    o_theirs = send(o_total[block_len:].astype(BF16), "far", 1)
    d_normed1 = scatter_4(e_keep, e_came, e_sides, e_other, block_len)
    d_input = d_middle + norm_backward(d_normed1, normed1, scale1)
    output = (middle + o_total[:block_len] + o_theirs.astype(F32)).astype(BF16)
    count = n_ctx // 2
    odd = position % 2
    gate, up = ffn_grad[:, :, :wide], ffn_grad[:, :, wide : 2 * wide]
    pieces = []
    for flip in range(2):
        pairs = [(c, ((c % 2) ^ flip) * count + c // 2) for c in range(n_ctx)]
        pieces.append(lax.ppermute(jnp.where(odd == flip, gate, up), CTX, pairs))
    down_grad = ffn_grad[:, :, 2 * wide : 2 * wide + share].transpose(0, 2, 1)
    down_grad = down_grad.reshape(n_far * share, quarter).astype(F32)
    upper = position >= count
    columns = [jnp.where(upper, pieces[1], pieces[0]), jnp.where(upper, pieces[0], pieces[1])]
    own_gain = lax.dynamic_slice_in_dim(gain2, (far * n_near + near) * quarter, quarter)
    gateup_grad = (
        jnp.concatenate([columns[i][f][:, :share] for i in range(2) for f in range(n_far)], axis=1).astype(F32)
        * own_gain[:, None]
    )
    sums, d_input, down_grad = meet(sums, d_input, down_grad)
    sums = exchange(sums, EVERY)
    sums, attn_grad, output, gateup_grad = meet(sums, attn_grad, output, gateup_grad)
    sums = jnp.sum(sums, axis=0)
    attn_grad = attn_grad.astype(F32)
    own_gain = lax.dynamic_slice_in_dim(gain1, (far * n_near + near) * quarter, quarter)
    qkv_grad = attn_grad[:, : q_cols + kv_cols] * own_gain[:, None]
    out_grad = attn_grad[:, q_cols + kv_cols :].T
    return (
        output.reshape(1, block_len, width),
        d_input.reshape(1, block_len, width),
        sums[0],
        qkv_grad[:, :q_cols],
        qkv_grad[:, q_cols:],
        out_grad,
        sums[1],
        sums[2],
        gateup_grad,
        down_grad,
    )


def solution(mesh):
    n_ctx, n_seq = mesh.shape["ctx"], mesh.shape["seq"]
    side = math.isqrt(n_ctx // 2)
    fine = Mesh(
        mesh.devices.reshape(n_ctx // 2 // side, side, 2, n_seq // 2, 2), EVERY
    )
    whole = P(EVERY)
    return jax.shard_map(
        per_device,
        mesh=fine,
        in_specs=(
            P(SEQ, CTX, None),
            P(SEQ, CTX, None),
            whole,
            whole,
            whole,
            whole,
            whole,
            whole,
            whole,
            whole,
        ),
        out_specs=(
            P(SEQ, CTX, None),
            P(SEQ, CTX, None),
            whole,
            P(SEQ, CTX),
            P(SEQ, CTX),
            P(CTX, SEQ),
            whole,
            whole,
            P(SEQ, CTX),
            P(CTX, SEQ),
        ),
        check_vma=False,
    )
```

```python
import functools
import math

import jax
import jax.numpy as jnp
from jax import lax
from jax.experimental import pallas as pl
from jax.experimental.pallas import tpu as pltpu
from jax.sharding import Mesh, PartitionSpec as P

NH = 10
HD = 256
FF = 7680
WINDOW = 2048

EPS = 1e-06
NEG = -1e30

F32 = jnp.float32
BF16 = jnp.bfloat16

CTX = ("hi", "lo", "core")
GROUP = ("hi", "lo", "core", "far")
SEQ = ("far", "near")
EVERY = ("hi", "lo", "core", "far", "near")


def dot(left, right):
    return jnp.dot(left, right, preferred_element_type=F32)


def dot_last(left, right):
    return lax.dot_general(left, right, (((1,), (1,)), ((), ())), preferred_element_type=F32)


def dot_first(left, right):
    return lax.dot_general(left, right, (((0,), (0,)), ((), ())), preferred_element_type=F32)


def send(value, axis, step):
    count = lax.axis_size(axis)
    return lax.ppermute(value, axis, [(i, (i + step) % count) for i in range(count)])


def meet(*values):
    return lax.optimization_barrier(values)


def side():
    return lax.axis_size("lo")


def send_cross(value, step, second):
    k = side()
    pairs = []
    for h in range(k):
        for l in range(k):
            for c in range(2):
                along_lo = (c == 0) != second
                to_h, to_l = (h, (l + step) % k) if along_lo else ((h + step) % k, l)
                pairs.append(((h * k + l) * 2 + c, (to_h * k + to_l) * 2 + c))
    return lax.ppermute(value, CTX, pairs)


def gather_0(block):
    return jnp.concatenate([block, send(block, "core", 1)])


def gather_1(pair):
    return [send_cross(pair, i, False) for i in range(1, side())]


def gather_2(sides):
    rows = sides[0].shape[0] // 2
    return [send_cross(value[:rows], j, True) for value in sides for j in range(1, side())]


def gather_3(pair, sides, corners):
    own = jnp.concatenate(sides + corners)
    return own, send(own, "core", 1)


def gather_all(pair, halves):
    rows = pair.shape[0] // 2
    return jnp.concatenate([pair[:rows], halves[0], pair[rows:], halves[1]])


def add(*values):
    return sum((value.astype(F32) for value in values[1:]), values[0].astype(F32))


def block_of(value, at, rows):
    k = side()
    value = value.reshape(-1, k * k, rows, value.shape[-1])[:, at]
    return value.reshape(-1, value.shape[-1])


def scatter_1(keep, came, rows):
    k = side()
    back = []
    for i in range(k - 1):
        for j in range(1, k):
            at = 2 * k - 1 + i * (k - 1) + j - 1
            low = add(block_of(keep, at, rows), block_of(came, at, rows)).astype(BF16)
            back.append(send_cross(low, -j, True))
    return back


def scatter_2(keep, came, back, rows):
    k = side()
    sides = []
    for i in range(1, k):
        first = add(block_of(keep, 2 * i - 1, rows), block_of(came, 2 * i - 1, rows))
        first = add(first, *back[(i - 1) * (k - 1) : i * (k - 1)])
        second = add(block_of(keep, 2 * i, rows), block_of(came, 2 * i, rows))
        sides.append(send_cross(jnp.concatenate([first, second]).astype(BF16), -i, False))
    return sides


def scatter_3(sides):
    half = sides[0].shape[0] // 2
    return send(add(*[value[half:] for value in sides]).astype(BF16), "core", 1)


def scatter_4(keep, came, sides, other, rows):
    half = sides[0].shape[0] // 2
    return add(
        block_of(keep, 0, rows), block_of(came, 0, rows), other, *[value[:half] for value in sides]
    )


def copy_blocks(order_ref, from_ref, to_ref):
    for n in range(to_ref.shape[0]):
        to_ref[n] = from_ref[order_ref[n]]


def pick_blocks(blocks, order):
    shape = order.shape + blocks.shape[1:]
    return pl.pallas_call(
        copy_blocks,
        out_shape=jax.ShapeDtypeStruct(shape, blocks.dtype),
        in_specs=[pl.BlockSpec(memory_space=pltpu.SMEM), pl.BlockSpec(memory_space=pltpu.VMEM)],
        out_specs=pl.BlockSpec(memory_space=pltpu.VMEM),
        cost_estimate=pl.CostEstimate(
            flops=0, bytes_accessed=2 * blocks.size * blocks.dtype.itemsize, transcendentals=0
        ),
        name="pick_blocks",
    )(order, blocks)


def order_ctx(by_device):
    k = side()
    h, l, c = (lax.axis_index(axis) for axis in CTX)
    picked = []
    for n in range(2 * k * k):
        if by_device:
            ih, il, ic = n // (2 * k), n // 2 % k, n % 2
            dh, dl = (h - ih) % k, (l - il) % k
            on_lo, on_hi = (dh == 0) & (dl != 0), (dl == 0) & (dh != 0)
            charge = jnp.where(on_lo, 0, jnp.where(on_hi, 1, ic))
            i, j = (dl, dh) if ic == 0 else (dh, dl)
            at = 2 * k - 1 + (i - 1) * (k - 1) + j - 1
            at = jnp.where(on_lo, 2 * dl - 1 + (ic != 0), jnp.where(on_hi, 2 * dh - 1 + (ic != 1), at))
            at = jnp.where((dh == 0) & (dl == 0), 0, at)
            source = jnp.where(charge == c, 0, k * k) + at
        else:
            other, at = n // (k * k), n % (k * k)
            charge = c ^ other
            if at == 0:
                i, j, core = 0, 0, charge
            elif at < 2 * k - 1:
                i, j, core = (at + 1) // 2, 0, charge ^ ((at + 1) % 2)
            else:
                i, j, core = (at - 2 * k + 1) // (k - 1) + 1, (at - 2 * k + 1) % (k - 1) + 1, charge
            dh, dl = jnp.where(charge == 0, j, i), jnp.where(charge == 0, i, j)
            source = ((h - dh) % k * k + (l - dl) % k) * 2 + core
        picked.append(source)
    return jnp.stack(picked).astype(jnp.int32)


def exchange(value, axes):
    return lax.all_to_all(value, axes, split_axis=0, concat_axis=0, tiled=True)


def dot_rows(left, right):
    return lax.dot_general(left, right, (((1,), (1,)), ((), ())), preferred_element_type=F32)


def middle_kernel(
    share, wide, order_ref, hidden_ref, d_first_ref, d_second_ref, gate_ref, up_ref, inner_ref, d_gu_ref, keep_ref, give_ref
):
    hidden = hidden_ref[...]
    gate = jnp.dot(hidden, gate_ref[...], preferred_element_type=F32)
    up = jnp.dot(hidden, up_ref[...], preferred_element_type=F32)
    d_inner = jnp.concatenate([d_first_ref[0], d_second_ref[0]]).astype(F32)
    root = (2.0 / math.pi) ** 0.5
    square = gate * gate
    bent = jnp.tanh(root * gate * (1.0 + 0.044715 * square))
    half = 0.5 * (1.0 + bent)
    gelu = gate * half
    slope = half + 0.5 * gate * (1.0 - bent * bent) * (root * (1.0 + 3 * 0.044715 * square))
    d_gate = (d_inner * up * slope).astype(BF16)
    d_up = (d_inner * gelu).astype(BF16)
    inner_ref[:, :share] = (gelu * up).astype(BF16)
    d_gu_ref[:, :share] = d_gate
    d_gu_ref[:, wide : wide + share] = d_up
    if wide > share:
        rest = jnp.zeros((hidden.shape[0], wide - share), BF16)
        inner_ref[:, share:] = rest
        d_gu_ref[:, share:wide] = rest
        d_gu_ref[:, wide + share :] = rest
    back = (dot_rows(d_gate, gate_ref[...]) + dot_rows(d_up, up_ref[...])).astype(BF16)
    step, steps = pl.program_id(0), pl.num_programs(0)

    @pl.when(step < steps // 2)
    def _():
        keep_ref[...] = back

    @pl.when(step >= steps // 2)
    def _():
        give_ref[...] = back


def feed_forward(hidden, d_inner, order, w_gate, w_up, wide):
    length, width = hidden.shape
    block, share = d_inner.shape[1:]
    rows = 2 * block
    steps = length // rows
    weight = pl.BlockSpec((width, share), lambda n, order_ref: (0, 0), pipeline_mode=pl.Buffered(1))
    return pl.pallas_call(
        functools.partial(middle_kernel, share, wide),
        out_shape=(
            jax.ShapeDtypeStruct((length, wide), BF16),
            jax.ShapeDtypeStruct((length, 2 * wide), BF16),
            jax.ShapeDtypeStruct((length // 2, width), BF16),
            jax.ShapeDtypeStruct((length // 2, width), BF16),
        ),
        grid_spec=pltpu.PrefetchScalarGridSpec(
            num_scalar_prefetch=1,
            grid=(steps,),
            in_specs=[
                pl.BlockSpec((rows, width), lambda n, order_ref: (n, 0)),
                pl.BlockSpec((1, block, share), lambda n, order_ref: (order_ref[2 * n], 0, 0)),
                pl.BlockSpec((1, block, share), lambda n, order_ref: (order_ref[2 * n + 1], 0, 0)),
                weight,
                weight,
            ],
            out_specs=[
                pl.BlockSpec((rows, wide), lambda n, order_ref: (n, 0)),
                pl.BlockSpec((rows, 2 * wide), lambda n, order_ref: (n, 0)),
                pl.BlockSpec((rows, width), lambda n, order_ref: (jnp.minimum(n, steps // 2 - 1), 0)),
                pl.BlockSpec((rows, width), lambda n, order_ref: (jnp.maximum(n - steps // 2, 0), 0)),
            ],
        ),
        compiler_params=pltpu.CompilerParams(vmem_limit_bytes=48 * 2**20),
        cost_estimate=pl.CostEstimate(
            flops=8 * length * width * share,
            bytes_accessed=4 * length * width + 4 * width * share,
            transcendentals=length * share,
        ),
        name="feed_forward",
    )(order, hidden, d_inner, d_inner, w_gate, w_up)


def gradient_kernel(both, hidden_ref, more_ref, final_ref, d_gu_ref, d_more_ref, inner_ref, grad_ref):
    grad_ref[0, 0, :, :both] = (
        dot_first(hidden_ref[...], d_gu_ref[...]) + dot_first(more_ref[...], d_more_ref[...])
    ).astype(BF16)
    grad_ref[0, 0, :, both:] = dot_first(final_ref[...], inner_ref[...]).astype(BF16)


def weight_gradients(hidden, d_gu, final, inner, n_far, n_near):
    length, width = hidden[0].shape
    quarter = width // (n_far * n_near)
    both, wide = d_gu[0].shape[1], inner.shape[1]
    rows = quarter if 16 * length * quarter <= 2**24 else 128
    steps = quarter // rows

    def columns(n, f, k):
        return (0, (f * n_near + n) * steps + k)

    def whole(value):
        return pl.BlockSpec(value.shape, lambda n, f, k: (0, 0), pipeline_mode=pl.Buffered(1))

    return pl.pallas_call(
        functools.partial(gradient_kernel, both),
        out_shape=jax.ShapeDtypeStruct((n_near, n_far, quarter, both + wide), BF16),
        grid=(n_near, n_far, steps),
        in_specs=[
            pl.BlockSpec((length, rows), columns),
            pl.BlockSpec((length, rows), columns),
            pl.BlockSpec((final.shape[0], rows), columns),
            whole(d_gu[0]),
            whole(d_gu[1]),
            whole(inner),
        ],
        out_specs=pl.BlockSpec((1, 1, rows, both + wide), lambda n, f, k: (n, f, k, 0)),
        compiler_params=pltpu.CompilerParams(vmem_limit_bytes=48 * 2**20),
        cost_estimate=pl.CostEstimate(
            flops=4 * length * width * (both + wide),
            bytes_accessed=8 * length * width + 2 * width * (both + wide),
            transcendentals=0,
        ),
        name="weight_gradients",
    )(*hidden, final, *d_gu, inner)


def two_gradients_kernel(left_ref, d_left_ref, right_ref, d_right_ref, grad_ref):
    split = d_left_ref.shape[1]
    grad_ref[:, :split] = dot_first(left_ref[...], d_left_ref[...]).astype(BF16)
    grad_ref[:, split:] = dot_first(right_ref[...], d_right_ref[...]).astype(BF16)


def two_gradients(left, d_left, right, d_right):
    length, width = left.shape
    rows = 256 if length <= 1024 else 128
    total = d_left.shape[1] + d_right.shape[1]

    def whole(value):
        return pl.BlockSpec(value.shape, lambda n: (0, 0), pipeline_mode=pl.Buffered(1))

    return pl.pallas_call(
        two_gradients_kernel,
        out_shape=jax.ShapeDtypeStruct((width, total), BF16),
        grid=(width // rows,),
        in_specs=[
            pl.BlockSpec((length, rows), lambda n: (0, n)),
            whole(d_left),
            pl.BlockSpec((length, rows), lambda n: (0, n)),
            whole(d_right),
        ],
        out_specs=pl.BlockSpec((rows, total), lambda n: (n, 0)),
        compiler_params=pltpu.CompilerParams(vmem_limit_bytes=32 * 2**20),
        cost_estimate=pl.CostEstimate(
            flops=2 * length * width * total,
            bytes_accessed=4 * length * width + 2 * width * total,
            transcendentals=0,
        ),
        name="two_gradients",
    )(left, d_left, right, d_right)


def norm_scale(value):
    return lax.rsqrt(jnp.mean(value * value, axis=-1, keepdims=True) + EPS)


def norm_backward(d_normed, normed, scale):
    return scale * (d_normed - normed * jnp.mean(d_normed * normed, axis=-1, keepdims=True))


def with_gain(weight, gain):
    return (weight.astype(F32) * gain.astype(F32)[:, None]).astype(BF16)


def in_place(mine, other, at):
    both = jnp.zeros(mine.shape[:1] + (2,) + mine.shape[1:], mine.dtype)
    rest = (0,) * (mine.ndim - 1)
    both = lax.dynamic_update_slice(both, mine[:, None], (0, at) + rest)
    return lax.dynamic_update_slice(both, other[:, None], (0, 1 - at) + rest)


def per_device(
    tokens, cotangent, gain_attn, w_query, w_keyval, w_out, b_out, gain_ffn, w_gateup, w_down
):
    block_len, width = tokens.shape[1:]
    n_ctx = lax.axis_size("hi") * lax.axis_size("lo") * lax.axis_size("core")
    n_far, n_near = lax.axis_size("far"), lax.axis_size("near")
    n_seq = n_far * n_near
    n_all = n_ctx * n_seq
    n_group = n_ctx * n_far
    rows = w_query.shape[0]
    length = n_ctx * block_len
    q_scale = HD ** (-0.5)
    position = (lax.axis_index("hi") * lax.axis_size("lo") + lax.axis_index("lo")) * 2 + lax.axis_index("core")
    far, near = lax.axis_index("far"), lax.axis_index("near")
    q_cols = NH * HD // n_ctx
    kv_cols = 2 * HD // n_ctx
    share = FF // n_group
    quarter = width // n_seq

    block = tokens.reshape(block_len, width)
    d_final = cotangent.reshape(block_len, width)
    residual = block.astype(F32)

    qkv_send = jnp.concatenate(
        [
            with_gain(w_query, gain_attn).reshape(rows, n_ctx, q_cols),
            with_gain(w_keyval, gain_attn).reshape(rows, n_ctx, kv_cols),
        ],
        axis=2,
    ).transpose(1, 0, 2)
    qkv_send = jnp.broadcast_to(qkv_send[:, None], (n_ctx, n_seq) + qkv_send.shape[1:])
    scale1 = norm_scale(residual)
    normed1 = residual * scale1
    vectors = jnp.stack([gain_attn, b_out, gain_ffn])
    vectors = jnp.pad(vectors, ((0, 5), (0, width - rows)))
    out_send = jnp.concatenate([w_out, vectors])[None]
    out_near = send(out_send, "near", 1)
    down_other = send(w_down, "near", 1)
    out_far = send(out_send, "far", 1)
    out_both = lax.ppermute(out_send, SEQ, [(i, (i + n_near) % n_seq ^ 1) for i in range(n_seq)])
    hidden1 = lax.all_gather(normed1.astype(BF16), CTX, axis=0, tiled=True)
    w_qkv = exchange(qkv_send.reshape((n_all,) + qkv_send.shape[2:]), EVERY)
    gateup_send = with_gain(w_gateup, gain_ffn).reshape(rows, 2, n_group, share).transpose(1, 2, 0, 3)

    hidden1, w_qkv, gateup_send, out_near, out_far, out_both, d_start, down_other = meet(
        hidden1,
        w_qkv.reshape(width, q_cols + kv_cols),
        gateup_send,
        out_near,
        out_far,
        out_both,
        d_final,
        down_other,
    )
    gate_half = exchange(gateup_send[0], GROUP)
    f_theirs = send(d_start, "far", 1)

    def along_seq(part):
        mine = in_place(part(out_send), part(out_near), near)
        other = in_place(part(out_far), part(out_both), near)
        return in_place(mine, other, far)

    out_rows = along_seq(lambda value: value[:, :rows]).reshape(n_seq * rows, width)
    vectors = along_seq(lambda value: value[:, rows : rows + 3, :rows]).reshape(-1)
    full_out = lax.all_gather(out_rows, CTX, axis=0, tiled=True)

    qkv = dot(hidden1, w_qkv)
    qkv = jnp.concatenate([qkv[:, :q_cols] * q_scale, qkv[:, q_cols:]], axis=1).astype(BF16)
    qkv = qkv.reshape(n_ctx, block_len, q_cols + kv_cols)
    kv_send = qkv[:, :, q_cols:].transpose(1, 0, 2).reshape(block_len, 2 * HD)
    kv_send = jnp.broadcast_to(kv_send[None], (n_ctx, block_len, 2 * HD))
    spare = block_len * 8 - n_seq * 3 * rows
    extra = jnp.concatenate([vectors, jnp.zeros((spare,), BF16)]).reshape(1, block_len, 8)
    extra = jnp.broadcast_to(extra, (n_ctx, block_len, 8))
    q_send = jnp.concatenate([qkv[:, :, :q_cols], kv_send, extra], axis=2)
    q_send, gate_half = meet(q_send, gate_half)
    came = exchange(q_send, CTX)
    gate_other = send(gate_half, "near", 1)
    came, up_send = meet(came, gateup_send[1])
    cut = -(-rows * 3 // 5 // 16) * 16
    up_first = exchange(up_send[:, :cut], GROUP)
    vectors = came[:, :, q_cols + 2 * HD :].reshape(n_ctx, -1)[:, : n_seq * 3 * rows]
    vectors = vectors.reshape(n_ctx * n_seq, 3, rows).transpose(1, 0, 2).reshape(3, width).astype(F32)
    gain1, bias, gain2 = vectors[0], vectors[1], vectors[2]
    query = came[:, :, :q_cols].transpose(1, 0, 2).reshape(block_len, NH, HD)
    keyval = came[:, :, q_cols : q_cols + 2 * HD].reshape(n_ctx, block_len, n_ctx, kv_cols).transpose(2, 1, 0, 3)
    keyval = keyval.reshape(length, 2 * HD)
    key, value = keyval[:, :HD], keyval[:, HD:]
    spacing = (position * block_len + jnp.arange(block_len, dtype=jnp.int32))[:, None] - jnp.arange(
        length, dtype=jnp.int32
    )[None, :]
    allowed = (spacing >= 0) & (spacing < WINDOW)
    scores = jnp.einsum("qhd,kd->hqk", query, key, preferred_element_type=F32)
    scores = jnp.where(allowed[None], scores, NEG)
    maximum = jnp.max(scores, axis=-1, keepdims=True)
    log_total = maximum + jnp.log(jnp.sum(jnp.exp(scores - maximum), axis=-1, keepdims=True))
    probs_low = jnp.exp(scores - log_total).astype(BF16)
    mixed = jnp.einsum("hqk,kd->qhd", probs_low, value, preferred_element_type=F32).astype(BF16)
    mixed = mixed.reshape(block_len, NH * HD)

    mixed, f_theirs, full_out, gate_other, up_first, up_send = meet(
        mixed, f_theirs, full_out, gate_other, up_first, up_send
    )
    up_second = exchange(up_send[:, cut:], GROUP)
    near_first = send(up_first, "near", 1)
    final_rows = lax.all_gather(jnp.concatenate([d_start, f_theirs]), CTX, axis=0, tiled=True)
    middle = residual + dot(mixed, full_out) + bias

    scale2 = norm_scale(middle)
    normed2 = middle * scale2
    hidden2 = normed2.astype(BF16)
    hidden2, up_second = meet(hidden2, up_second)
    m_pair = gather_0(hidden2)
    theirs = send(hidden2, "far", 1)
    near_second = send(up_second, "near", 1)
    m_sides = gather_1(m_pair)
    w_dn = in_place(w_down[None], down_other[None], near).reshape(share, width)
    devices = order_ctx(False)
    w_gate = in_place(gate_half, gate_other, near).reshape(width, share)
    m_sides, theirs, near_first, w_dn, w_gate = meet(m_sides, theirs, near_first, w_dn, w_gate)
    m_corners = gather_2(m_sides)
    t_pair = gather_0(theirs)
    m_corners, t_pair, near_second = meet(m_corners, t_pair, near_second)
    d_inner = dot_last(final_rows, w_dn).astype(BF16).reshape(2 * n_ctx, block_len, share)
    m_halves = gather_3(m_pair, m_sides, m_corners)
    t_sides = gather_1(t_pair)
    up_half = jnp.concatenate([up_first, up_second], axis=1)
    up_other = jnp.concatenate([near_first, near_second], axis=1)
    w_up = in_place(up_half, up_other, near).reshape(width, share)
    m_halves, t_sides, w_up, d_inner = meet(m_halves, t_sides, w_up, d_inner)
    t_corners = gather_2(t_sides)
    hidden_m = gather_all(m_pair, m_halves)
    t_corners, hidden_m = meet(t_corners, hidden_m)
    t_halves = gather_3(t_pair, t_sides, t_corners)

    wide = -(-share // 128) * 128
    half = length // 2
    mixed_send = mixed.reshape(block_len, n_ctx, q_cols).transpose(1, 0, 2)
    mixed_send, t_halves = meet(mixed_send, t_halves)
    mixed_cols = exchange(mixed_send, CTX)
    inner_m, d_gu_m, m_keep, m_give = feed_forward(hidden_m, d_inner, 2 * devices, w_gate, w_up, wide)
    m_give, t_halves = meet(m_give, t_halves)
    m_came = send(m_give, "core", 1)
    hidden_t = gather_all(t_pair, t_halves)
    inner_t, d_gu_t, t_keep, t_give = feed_forward(hidden_t, d_inner, 2 * devices + 1, w_gate, w_up, wide)
    t_give, m_keep, m_came, mixed_cols, inner_m = meet(t_give, m_keep, m_came, mixed_cols, inner_m)
    t_came = send(t_give, "core", 1)
    m_back = scatter_1(m_keep, m_came, block_len)
    places = order_ctx(True)
    inner_rows = jnp.concatenate([inner_m, inner_t]).reshape(2 * n_ctx, block_len, wide)
    inner_rows = pick_blocks(inner_rows, jnp.stack([places, places + n_ctx], axis=1).reshape(-1))
    inner_rows, t_keep, t_came, m_back, m_keep, m_came, inner_m, inner_t = meet(
        inner_rows, t_keep, t_came, m_back, m_keep, m_came, inner_m, inner_t
    )
    t_back = scatter_1(t_keep, t_came, block_len)
    m_sides = scatter_2(m_keep, m_came, m_back, block_len)
    out_give = dot(jnp.concatenate([inner_m[half:, :share], inner_t[half:, :share]]), w_dn).astype(BF16)
    out_keep = dot(jnp.concatenate([inner_m[:half, :share], inner_t[:half, :share]]), w_dn).astype(BF16)
    out_give, out_keep, t_back, t_keep, t_came, d_gu_m, d_gu_t = meet(
        out_give, out_keep, t_back, t_keep, t_came, d_gu_m, d_gu_t
    )
    t_sides = scatter_2(t_keep, t_came, t_back, block_len)

    ffn_grad = weight_gradients(
        (hidden_m, hidden_t),
        (d_gu_m, d_gu_t),
        final_rows,
        inner_rows.reshape(2 * length, wide),
        n_far,
        n_near,
    )
    ffn_grad, t_sides, m_sides, t_keep, t_came = meet(ffn_grad, t_sides, m_sides, t_keep, t_came)
    t_other = scatter_3(t_sides)
    m_other = scatter_3(m_sides)
    theirs = scatter_4(t_keep, t_came, t_sides, t_other, block_len).astype(BF16)
    theirs = send(theirs, "far", 1)
    m_other, theirs = meet(m_other, theirs)
    ffn_grad = lax.psum_scatter(ffn_grad, "near", scatter_dimension=0, tiled=True)
    d_hidden2 = scatter_4(m_keep, m_came, m_sides, m_other, block_len) + theirs.astype(F32)

    d_middle = d_final.astype(F32) + norm_backward(d_hidden2, normed2, scale2)
    d_gain2 = jnp.sum(d_hidden2 * normed2, axis=0) / gain2
    d_bias = jnp.sum(d_middle, axis=0)
    d_low = d_middle.astype(BF16)
    d_low, out_give = meet(d_low, out_give)
    l_pair = gather_0(d_low)
    l_pair, d_low, out_give = meet(l_pair, d_low, out_give)
    l_sides = gather_1(l_pair)
    o_came = send(out_give, "core", 1)
    d_mixed = dot_last(d_low, full_out).astype(BF16)
    d_mixed, o_came = meet(d_mixed, o_came)
    o_back = scatter_1(out_keep, o_came, block_len)
    d_mixed = d_mixed.reshape(block_len, NH, HD)
    scores = jnp.einsum("qhd,kd->hqk", query, key, preferred_element_type=F32)
    scores = jnp.where(allowed[None], scores, NEG)
    probs = jnp.exp(scores - log_total)
    probs_again = probs.astype(BF16)
    d_probs = jnp.einsum("qhd,kd->hqk", d_mixed, value, preferred_element_type=F32)
    delta = jnp.sum(probs * d_probs, axis=-1, keepdims=True)
    d_scores = (probs * (d_probs - delta)).astype(BF16)
    d_query = jnp.einsum("hqk,kd->qhd", d_scores, key, preferred_element_type=F32) * q_scale
    d_key = jnp.einsum("hqk,qhd->kd", d_scores, query, preferred_element_type=F32)
    d_value = jnp.einsum("hqk,qhd->kd", probs_again, d_mixed, preferred_element_type=F32)
    d_query = d_query.reshape(block_len, n_ctx, q_cols).astype(BF16).transpose(1, 0, 2)
    d_keyval = jnp.concatenate([d_key, d_value], axis=1).astype(BF16)
    d_keyval = d_keyval.reshape(n_ctx, block_len, n_ctx, kv_cols).transpose(2, 1, 0, 3)
    d_keyval = d_keyval.reshape(n_ctx, block_len, 2 * HD)
    d_send = jnp.concatenate([d_query, d_keyval], axis=2)
    d_send, l_sides, o_back, out_keep, o_came, mixed_cols = meet(
        d_send, l_sides, o_back, out_keep, o_came, mixed_cols
    )
    came = exchange(d_send, CTX)
    l_corners = gather_2(l_sides)
    o_sides = scatter_2(out_keep, o_came, o_back, block_len)
    mixed_cols = pick_blocks(mixed_cols, devices).reshape(length, q_cols)
    came, l_corners, ffn_grad, mixed_cols = meet(came, l_corners, ffn_grad, mixed_cols)
    ffn_grad = exchange(ffn_grad[0], ("far",))
    l_halves = gather_3(l_pair, l_sides, l_corners)
    d_keyval = jnp.sum(came[:, :, q_cols:].astype(F32), axis=0).astype(BF16)
    d_keyval = d_keyval.reshape(block_len, n_ctx, kv_cols).transpose(1, 0, 2)
    d_qkv = jnp.concatenate([came[:, :, :q_cols], d_keyval], axis=2)
    d_back = pick_blocks(d_qkv, devices).reshape(length, q_cols + kv_cols)
    d_qkv = d_qkv.reshape(length, q_cols + kv_cols)
    e_came = send(dot_last(d_back[half:], w_qkv).astype(BF16), "core", 1)
    e_keep = dot_last(d_back[:half], w_qkv).astype(BF16)
    e_keep, e_came, l_halves, o_sides, d_qkv = meet(e_keep, e_came, l_halves, o_sides, d_qkv)
    e_back = scatter_1(e_keep, e_came, block_len)
    o_other = scatter_3(o_sides)
    attn_grad = two_gradients(hidden1, d_qkv, gather_all(l_pair, l_halves), mixed_cols)
    d_gain1 = attn_grad[:, : q_cols + kv_cols].astype(F32) * w_qkv.astype(F32)
    d_gain1 = jnp.sum(d_gain1, axis=1) / gain1
    e_back, o_other, out_keep, o_came = meet(e_back, o_other, out_keep, o_came)
    e_sides = scatter_2(e_keep, e_came, e_back, block_len)
    sums = jnp.stack([d_gain1, d_bias, d_gain2]).reshape(3, n_all, rows).transpose(1, 0, 2)
    e_sides, attn_grad, sums, ffn_grad = meet(e_sides, attn_grad, sums, ffn_grad)
    attn_grad = lax.psum_scatter(attn_grad, SEQ, scatter_dimension=0, tiled=True)
    e_other = scatter_3(e_sides)
    o_total = scatter_4(out_keep, o_came, o_sides, o_other, block_len)
    o_theirs = send(o_total[block_len:].astype(BF16), "far", 1)
    d_normed1 = scatter_4(e_keep, e_came, e_sides, e_other, block_len)
    d_input = d_middle + norm_backward(d_normed1, normed1, scale1)
    output = (middle + o_total[:block_len] + o_theirs.astype(F32)).astype(BF16)
    count = n_ctx // 2
    odd = position % 2
    gate, up = ffn_grad[:, :, :wide], ffn_grad[:, :, wide : 2 * wide]
    pieces = []
    for flip in range(2):
        pairs = [(c, ((c % 2) ^ flip) * count + c // 2) for c in range(n_ctx)]
        pieces.append(lax.ppermute(jnp.where(odd == flip, gate, up), CTX, pairs))
    down_grad = ffn_grad[:, :, 2 * wide : 2 * wide + share].transpose(0, 2, 1)
    down_grad = down_grad.reshape(n_far * share, quarter).astype(F32)
    upper = position >= count
    columns = [jnp.where(upper, pieces[1], pieces[0]), jnp.where(upper, pieces[0], pieces[1])]
    own_gain = lax.dynamic_slice_in_dim(gain2, (far * n_near + near) * quarter, quarter)
    gateup_grad = (
        jnp.concatenate([columns[i][f][:, :share] for i in range(2) for f in range(n_far)], axis=1).astype(F32)
        * own_gain[:, None]
    )
    sums, d_input, down_grad = meet(sums, d_input, down_grad)
    sums = exchange(sums, EVERY)
    sums, attn_grad, output, gateup_grad = meet(sums, attn_grad, output, gateup_grad)
    sums = jnp.sum(sums, axis=0)
    attn_grad = attn_grad.astype(F32)
    own_gain = lax.dynamic_slice_in_dim(gain1, (far * n_near + near) * quarter, quarter)
    qkv_grad = attn_grad[:, : q_cols + kv_cols] * own_gain[:, None]
    out_grad = attn_grad[:, q_cols + kv_cols :].T
    return (
        output.reshape(1, block_len, width),
        d_input.reshape(1, block_len, width),
        sums[0],
        qkv_grad[:, :q_cols],
        qkv_grad[:, q_cols:],
        out_grad,
        sums[1],
        sums[2],
        gateup_grad,
        down_grad,
    )


def solution(mesh):
    n_ctx, n_seq = mesh.shape["ctx"], mesh.shape["seq"]
    side = math.isqrt(n_ctx // 2)
    fine = Mesh(
        mesh.devices.reshape(n_ctx // 2 // side, side, 2, n_seq // 2, 2), EVERY
    )
    whole = P(EVERY)
    return jax.shard_map(
        per_device,
        mesh=fine,
        in_specs=(
            P(SEQ, CTX, None),
            P(SEQ, CTX, None),
            whole,
            whole,
            whole,
            whole,
            whole,
            whole,
            whole,
            whole,
        ),
        out_specs=(
            P(SEQ, CTX, None),
            P(SEQ, CTX, None),
            whole,
            P(SEQ, CTX),
            P(SEQ, CTX),
            P(CTX, SEQ),
            whole,
            whole,
            P(SEQ, CTX),
            P(CTX, SEQ),
        ),
        check_vma=False,
    )
```

```python
import functools
import math

import jax
import jax.numpy as jnp
from jax import lax
from jax.experimental import pallas as pl
from jax.experimental.pallas import tpu as pltpu
from jax.sharding import Mesh, PartitionSpec as P

NH = 10
HD = 256
FF = 7680
WINDOW = 2048

EPS = 1e-06
NEG = -1e30

F32 = jnp.float32
BF16 = jnp.bfloat16

CTX = ("hi", "lo", "core")
GROUP = ("hi", "lo", "core", "far")
SEQ = ("far", "near")
EVERY = ("hi", "lo", "core", "far", "near")


def dot(left, right):
    return jnp.dot(left, right, preferred_element_type=F32)


def dot_last(left, right):
    return lax.dot_general(left, right, (((1,), (1,)), ((), ())), preferred_element_type=F32)


def dot_first(left, right):
    return lax.dot_general(left, right, (((0,), (0,)), ((), ())), preferred_element_type=F32)


def send(value, axis, step):
    count = lax.axis_size(axis)
    return lax.ppermute(value, axis, [(i, (i + step) % count) for i in range(count)])


def meet(*values):
    return lax.optimization_barrier(values)


def side():
    return lax.axis_size("lo")


def send_cross(value, step, second):
    k = side()
    pairs = []
    for h in range(k):
        for l in range(k):
            for c in range(2):
                along_lo = (c == 0) != second
                to_h, to_l = (h, (l + step) % k) if along_lo else ((h + step) % k, l)
                pairs.append(((h * k + l) * 2 + c, (to_h * k + to_l) * 2 + c))
    return lax.ppermute(value, CTX, pairs)


def gather_0(block):
    return jnp.concatenate([block, send(block, "core", 1)])


def gather_1(pair):
    return [send_cross(pair, i, False) for i in range(1, side())]


def gather_2(sides):
    rows = sides[0].shape[0] // 2
    return [send_cross(value[:rows], j, True) for value in sides for j in range(1, side())]


def gather_3(pair, sides, corners):
    own = jnp.concatenate(sides + corners)
    return own, send(own, "core", 1)


def gather_all(pair, halves):
    rows = pair.shape[0] // 2
    return jnp.concatenate([pair[:rows], halves[0], pair[rows:], halves[1]])


def add(*values):
    return sum((value.astype(F32) for value in values[1:]), values[0].astype(F32))


def block_of(value, at, rows):
    k = side()
    value = value.reshape(-1, k * k, rows, value.shape[-1])[:, at]
    return value.reshape(-1, value.shape[-1])


def scatter_1(keep, came, rows):
    k = side()
    back = []
    for i in range(k - 1):
        for j in range(1, k):
            at = 2 * k - 1 + i * (k - 1) + j - 1
            low = add(block_of(keep, at, rows), block_of(came, at, rows)).astype(BF16)
            back.append(send_cross(low, -j, True))
    return back


def scatter_2(keep, came, back, rows):
    k = side()
    sides = []
    for i in range(1, k):
        first = add(block_of(keep, 2 * i - 1, rows), block_of(came, 2 * i - 1, rows))
        first = add(first, *back[(i - 1) * (k - 1) : i * (k - 1)])
        second = add(block_of(keep, 2 * i, rows), block_of(came, 2 * i, rows))
        sides.append(send_cross(jnp.concatenate([first, second]).astype(BF16), -i, False))
    return sides


def scatter_3(sides):
    half = sides[0].shape[0] // 2
    return send(add(*[value[half:] for value in sides]).astype(BF16), "core", 1)


def scatter_4(keep, came, sides, other, rows):
    half = sides[0].shape[0] // 2
    return add(
        block_of(keep, 0, rows), block_of(came, 0, rows), other, *[value[:half] for value in sides]
    )


def copy_blocks(order_ref, from_ref, to_ref):
    for n in range(to_ref.shape[0]):
        to_ref[n] = from_ref[order_ref[n]]


def pick_blocks(blocks, order):
    shape = order.shape + blocks.shape[1:]
    return pl.pallas_call(
        copy_blocks,
        out_shape=jax.ShapeDtypeStruct(shape, blocks.dtype),
        in_specs=[pl.BlockSpec(memory_space=pltpu.SMEM), pl.BlockSpec(memory_space=pltpu.VMEM)],
        out_specs=pl.BlockSpec(memory_space=pltpu.VMEM),
        cost_estimate=pl.CostEstimate(
            flops=0, bytes_accessed=2 * blocks.size * blocks.dtype.itemsize, transcendentals=0
        ),
        name="pick_blocks",
    )(order, blocks)


def order_ctx(by_device):
    k = side()
    h, l, c = (lax.axis_index(axis) for axis in CTX)
    picked = []
    for n in range(2 * k * k):
        if by_device:
            ih, il, ic = n // (2 * k), n // 2 % k, n % 2
            dh, dl = (h - ih) % k, (l - il) % k
            on_lo, on_hi = (dh == 0) & (dl != 0), (dl == 0) & (dh != 0)
            charge = jnp.where(on_lo, 0, jnp.where(on_hi, 1, ic))
            i, j = (dl, dh) if ic == 0 else (dh, dl)
            at = 2 * k - 1 + (i - 1) * (k - 1) + j - 1
            at = jnp.where(on_lo, 2 * dl - 1 + (ic != 0), jnp.where(on_hi, 2 * dh - 1 + (ic != 1), at))
            at = jnp.where((dh == 0) & (dl == 0), 0, at)
            source = jnp.where(charge == c, 0, k * k) + at
        else:
            other, at = n // (k * k), n % (k * k)
            charge = c ^ other
            if at == 0:
                i, j, core = 0, 0, charge
            elif at < 2 * k - 1:
                i, j, core = (at + 1) // 2, 0, charge ^ ((at + 1) % 2)
            else:
                i, j, core = (at - 2 * k + 1) // (k - 1) + 1, (at - 2 * k + 1) % (k - 1) + 1, charge
            dh, dl = jnp.where(charge == 0, j, i), jnp.where(charge == 0, i, j)
            source = ((h - dh) % k * k + (l - dl) % k) * 2 + core
        picked.append(source)
    return jnp.stack(picked).astype(jnp.int32)


def exchange(value, axes):
    return lax.all_to_all(value, axes, split_axis=0, concat_axis=0, tiled=True)


def dot_rows(left, right):
    return lax.dot_general(left, right, (((1,), (1,)), ((), ())), preferred_element_type=F32)


def middle_kernel(
    share, wide, order_ref, hidden_ref, d_first_ref, d_second_ref, gate_ref, up_ref, inner_ref, d_gu_ref, keep_ref, give_ref
):
    hidden = hidden_ref[...]
    gate = jnp.dot(hidden, gate_ref[...], preferred_element_type=F32)
    up = jnp.dot(hidden, up_ref[...], preferred_element_type=F32)
    d_inner = jnp.concatenate([d_first_ref[0], d_second_ref[0]]).astype(F32)
    root = (2.0 / math.pi) ** 0.5
    square = gate * gate
    bent = jnp.tanh(root * gate * (1.0 + 0.044715 * square))
    half = 0.5 * (1.0 + bent)
    gelu = gate * half
    slope = half + 0.5 * gate * (1.0 - bent * bent) * (root * (1.0 + 3 * 0.044715 * square))
    d_gate = (d_inner * up * slope).astype(BF16)
    d_up = (d_inner * gelu).astype(BF16)
    inner_ref[:, :share] = (gelu * up).astype(BF16)
    d_gu_ref[:, :share] = d_gate
    d_gu_ref[:, wide : wide + share] = d_up
    if wide > share:
        rest = jnp.zeros((hidden.shape[0], wide - share), BF16)
        inner_ref[:, share:] = rest
        d_gu_ref[:, share:wide] = rest
        d_gu_ref[:, wide + share :] = rest
    back = (dot_rows(d_gate, gate_ref[...]) + dot_rows(d_up, up_ref[...])).astype(BF16)
    step, steps = pl.program_id(0), pl.num_programs(0)

    @pl.when(step < steps // 2)
    def _():
        keep_ref[...] = back

    @pl.when(step >= steps // 2)
    def _():
        give_ref[...] = back


def feed_forward(hidden, d_inner, order, w_gate, w_up, wide):
    length, width = hidden.shape
    block, share = d_inner.shape[1:]
    rows = 2 * block
    steps = length // rows
    weight = pl.BlockSpec((width, share), lambda n, order_ref: (0, 0), pipeline_mode=pl.Buffered(1))
    return pl.pallas_call(
        functools.partial(middle_kernel, share, wide),
        out_shape=(
            jax.ShapeDtypeStruct((length, wide), BF16),
            jax.ShapeDtypeStruct((length, 2 * wide), BF16),
            jax.ShapeDtypeStruct((length // 2, width), BF16),
            jax.ShapeDtypeStruct((length // 2, width), BF16),
        ),
        grid_spec=pltpu.PrefetchScalarGridSpec(
            num_scalar_prefetch=1,
            grid=(steps,),
            in_specs=[
                pl.BlockSpec((rows, width), lambda n, order_ref: (n, 0)),
                pl.BlockSpec((1, block, share), lambda n, order_ref: (order_ref[2 * n], 0, 0)),
                pl.BlockSpec((1, block, share), lambda n, order_ref: (order_ref[2 * n + 1], 0, 0)),
                weight,
                weight,
            ],
            out_specs=[
                pl.BlockSpec((rows, wide), lambda n, order_ref: (n, 0)),
                pl.BlockSpec((rows, 2 * wide), lambda n, order_ref: (n, 0)),
                pl.BlockSpec((rows, width), lambda n, order_ref: (jnp.minimum(n, steps // 2 - 1), 0)),
                pl.BlockSpec((rows, width), lambda n, order_ref: (jnp.maximum(n - steps // 2, 0), 0)),
            ],
        ),
        compiler_params=pltpu.CompilerParams(vmem_limit_bytes=48 * 2**20),
        cost_estimate=pl.CostEstimate(
            flops=8 * length * width * share,
            bytes_accessed=4 * length * width + 4 * width * share,
            transcendentals=length * share,
        ),
        name="feed_forward",
    )(order, hidden, d_inner, d_inner, w_gate, w_up)


def gradient_kernel(both, hidden_ref, more_ref, final_ref, d_gu_ref, d_more_ref, inner_ref, grad_ref):
    grad_ref[0, 0, :, :both] = (
        dot_first(hidden_ref[...], d_gu_ref[...]) + dot_first(more_ref[...], d_more_ref[...])
    ).astype(BF16)
    grad_ref[0, 0, :, both:] = dot_first(final_ref[...], inner_ref[...]).astype(BF16)


def weight_gradients(hidden, d_gu, final, inner, n_far, n_near):
    length, width = hidden[0].shape
    quarter = width // (n_far * n_near)
    both, wide = d_gu[0].shape[1], inner.shape[1]
    rows = quarter if 16 * length * quarter <= 2**24 else 128
    steps = quarter // rows

    def columns(n, f, k):
        return (0, (f * n_near + n) * steps + k)

    def whole(value):
        return pl.BlockSpec(value.shape, lambda n, f, k: (0, 0), pipeline_mode=pl.Buffered(1))

    return pl.pallas_call(
        functools.partial(gradient_kernel, both),
        out_shape=jax.ShapeDtypeStruct((n_near, n_far, quarter, both + wide), BF16),
        grid=(n_near, n_far, steps),
        in_specs=[
            pl.BlockSpec((length, rows), columns),
            pl.BlockSpec((length, rows), columns),
            pl.BlockSpec((final.shape[0], rows), columns),
            whole(d_gu[0]),
            whole(d_gu[1]),
            whole(inner),
        ],
        out_specs=pl.BlockSpec((1, 1, rows, both + wide), lambda n, f, k: (n, f, k, 0)),
        compiler_params=pltpu.CompilerParams(vmem_limit_bytes=48 * 2**20),
        cost_estimate=pl.CostEstimate(
            flops=4 * length * width * (both + wide),
            bytes_accessed=8 * length * width + 2 * width * (both + wide),
            transcendentals=0,
        ),
        name="weight_gradients",
    )(*hidden, final, *d_gu, inner)


def two_gradients_kernel(left_ref, d_left_ref, right_ref, d_right_ref, grad_ref):
    split = d_left_ref.shape[1]
    grad_ref[:, :split] = dot_first(left_ref[...], d_left_ref[...]).astype(BF16)
    grad_ref[:, split:] = dot_first(right_ref[...], d_right_ref[...]).astype(BF16)


def two_gradients(left, d_left, right, d_right):
    length, width = left.shape
    rows = 256 if length <= 1024 else 128
    total = d_left.shape[1] + d_right.shape[1]

    def whole(value):
        return pl.BlockSpec(value.shape, lambda n: (0, 0), pipeline_mode=pl.Buffered(1))

    return pl.pallas_call(
        two_gradients_kernel,
        out_shape=jax.ShapeDtypeStruct((width, total), BF16),
        grid=(width // rows,),
        in_specs=[
            pl.BlockSpec((length, rows), lambda n: (0, n)),
            whole(d_left),
            pl.BlockSpec((length, rows), lambda n: (0, n)),
            whole(d_right),
        ],
        out_specs=pl.BlockSpec((rows, total), lambda n: (n, 0)),
        compiler_params=pltpu.CompilerParams(vmem_limit_bytes=32 * 2**20),
        cost_estimate=pl.CostEstimate(
            flops=2 * length * width * total,
            bytes_accessed=4 * length * width + 2 * width * total,
            transcendentals=0,
        ),
        name="two_gradients",
    )(left, d_left, right, d_right)


def norm_scale(value):
    return lax.rsqrt(jnp.mean(value * value, axis=-1, keepdims=True) + EPS)


def norm_backward(d_normed, normed, scale):
    return scale * (d_normed - normed * jnp.mean(d_normed * normed, axis=-1, keepdims=True))


def with_gain(weight, gain):
    return (weight.astype(F32) * gain.astype(F32)[:, None]).astype(BF16)


def in_place(mine, other, at):
    both = jnp.zeros(mine.shape[:1] + (2,) + mine.shape[1:], mine.dtype)
    rest = (0,) * (mine.ndim - 1)
    both = lax.dynamic_update_slice(both, mine[:, None], (0, at) + rest)
    return lax.dynamic_update_slice(both, other[:, None], (0, 1 - at) + rest)


def per_device(
    tokens, cotangent, gain_attn, w_query, w_keyval, w_out, b_out, gain_ffn, w_gateup, w_down
):
    block_len, width = tokens.shape[1:]
    n_ctx = lax.axis_size("hi") * lax.axis_size("lo") * lax.axis_size("core")
    n_far, n_near = lax.axis_size("far"), lax.axis_size("near")
    n_seq = n_far * n_near
    n_all = n_ctx * n_seq
    n_group = n_ctx * n_far
    rows = w_query.shape[0]
    length = n_ctx * block_len
    q_scale = HD ** (-0.5)
    position = (lax.axis_index("hi") * lax.axis_size("lo") + lax.axis_index("lo")) * 2 + lax.axis_index("core")
    far, near = lax.axis_index("far"), lax.axis_index("near")
    q_cols = NH * HD // n_ctx
    kv_cols = 2 * HD // n_ctx
    share = FF // n_group
    quarter = width // n_seq

    block = tokens.reshape(block_len, width)
    d_final = cotangent.reshape(block_len, width)
    residual = block.astype(F32)

    qkv_send = jnp.concatenate(
        [
            with_gain(w_query, gain_attn).reshape(rows, n_ctx, q_cols),
            with_gain(w_keyval, gain_attn).reshape(rows, n_ctx, kv_cols),
        ],
        axis=2,
    ).transpose(1, 0, 2)
    qkv_send = jnp.broadcast_to(qkv_send[:, None], (n_ctx, n_seq) + qkv_send.shape[1:])
    scale1 = norm_scale(residual)
    normed1 = residual * scale1
    vectors = jnp.stack([gain_attn, b_out, gain_ffn])
    vectors = jnp.pad(vectors, ((0, 5), (0, width - rows)))
    out_send = jnp.concatenate([w_out, vectors])[None]
    out_near = send(out_send, "near", 1)
    down_other = send(w_down, "near", 1)
    out_far = send(out_send, "far", 1)
    out_both = lax.ppermute(out_send, SEQ, [(i, (i + n_near) % n_seq ^ 1) for i in range(n_seq)])
    hidden1 = lax.all_gather(normed1.astype(BF16), CTX, axis=0, tiled=True)
    w_qkv = exchange(qkv_send.reshape((n_all,) + qkv_send.shape[2:]), EVERY)
    gateup_send = with_gain(w_gateup, gain_ffn).reshape(rows, 2, n_group, share).transpose(1, 2, 0, 3)

    hidden1, w_qkv, gateup_send, out_near, out_far, out_both, d_start, down_other = meet(
        hidden1,
        w_qkv.reshape(width, q_cols + kv_cols),
        gateup_send,
        out_near,
        out_far,
        out_both,
        d_final,
        down_other,
    )
    gate_half = exchange(gateup_send[0], GROUP)
    f_theirs = send(d_start, "far", 1)

    def along_seq(part):
        mine = in_place(part(out_send), part(out_near), near)
        other = in_place(part(out_far), part(out_both), near)
        return in_place(mine, other, far)

    out_rows = along_seq(lambda value: value[:, :rows]).reshape(n_seq * rows, width)
    vectors = along_seq(lambda value: value[:, rows : rows + 3, :rows]).reshape(-1)
    full_out = lax.all_gather(out_rows, CTX, axis=0, tiled=True)

    qkv = dot(hidden1, w_qkv)
    qkv = jnp.concatenate([qkv[:, :q_cols] * q_scale, qkv[:, q_cols:]], axis=1).astype(BF16)
    qkv = qkv.reshape(n_ctx, block_len, q_cols + kv_cols)
    kv_send = qkv[:, :, q_cols:].transpose(1, 0, 2).reshape(block_len, 2 * HD)
    kv_send = jnp.broadcast_to(kv_send[None], (n_ctx, block_len, 2 * HD))
    spare = block_len * 8 - n_seq * 3 * rows
    extra = jnp.concatenate([vectors, jnp.zeros((spare,), BF16)]).reshape(1, block_len, 8)
    extra = jnp.broadcast_to(extra, (n_ctx, block_len, 8))
    q_send = jnp.concatenate([qkv[:, :, :q_cols], kv_send, extra], axis=2)
    q_send, gate_half = meet(q_send, gate_half)
    came = exchange(q_send, CTX)
    gate_other = send(gate_half, "near", 1)
    came, up_send = meet(came, gateup_send[1])
    cut = rows * 4 // 5 // 16 * 16
    up_first = exchange(up_send[:, :cut], GROUP)
    vectors = came[:, :, q_cols + 2 * HD :].reshape(n_ctx, -1)[:, : n_seq * 3 * rows]
    vectors = vectors.reshape(n_ctx * n_seq, 3, rows).transpose(1, 0, 2).reshape(3, width).astype(F32)
    gain1, bias, gain2 = vectors[0], vectors[1], vectors[2]
    query = came[:, :, :q_cols].transpose(1, 0, 2).reshape(block_len, NH, HD)
    keyval = came[:, :, q_cols : q_cols + 2 * HD].reshape(n_ctx, block_len, n_ctx, kv_cols).transpose(2, 1, 0, 3)
    keyval = keyval.reshape(length, 2 * HD)
    key, value = keyval[:, :HD], keyval[:, HD:]
    spacing = (position * block_len + jnp.arange(block_len, dtype=jnp.int32))[:, None] - jnp.arange(
        length, dtype=jnp.int32
    )[None, :]
    allowed = (spacing >= 0) & (spacing < WINDOW)
    scores = jnp.einsum("qhd,kd->hqk", query, key, preferred_element_type=F32)
    scores = jnp.where(allowed[None], scores, NEG)
    maximum = jnp.max(scores, axis=-1, keepdims=True)
    log_total = maximum + jnp.log(jnp.sum(jnp.exp(scores - maximum), axis=-1, keepdims=True))
    probs_low = jnp.exp(scores - log_total).astype(BF16)
    mixed = jnp.einsum("hqk,kd->qhd", probs_low, value, preferred_element_type=F32).astype(BF16)
    mixed = mixed.reshape(block_len, NH * HD)

    mixed, f_theirs, full_out, gate_other, up_first, up_send = meet(
        mixed, f_theirs, full_out, gate_other, up_first, up_send
    )
    up_second = exchange(up_send[:, cut:], GROUP)
    near_first = send(up_first, "near", 1)
    final_rows = lax.all_gather(jnp.concatenate([d_start, f_theirs]), CTX, axis=0, tiled=True)
    middle = residual + dot(mixed, full_out) + bias

    scale2 = norm_scale(middle)
    normed2 = middle * scale2
    hidden2 = normed2.astype(BF16)
    hidden2, up_second = meet(hidden2, up_second)
    m_pair = gather_0(hidden2)
    theirs = send(hidden2, "far", 1)
    near_second = send(up_second, "near", 1)
    m_sides = gather_1(m_pair)
    w_dn = in_place(w_down[None], down_other[None], near).reshape(share, width)
    devices = order_ctx(False)
    w_gate = in_place(gate_half, gate_other, near).reshape(width, share)
    m_sides, theirs, near_first, w_dn, w_gate = meet(m_sides, theirs, near_first, w_dn, w_gate)
    m_corners = gather_2(m_sides)
    t_pair = gather_0(theirs)
    m_corners, t_pair, near_second = meet(m_corners, t_pair, near_second)
    d_inner = dot_last(final_rows, w_dn).astype(BF16).reshape(2 * n_ctx, block_len, share)
    m_halves = gather_3(m_pair, m_sides, m_corners)
    t_sides = gather_1(t_pair)
    up_half = jnp.concatenate([up_first, up_second], axis=1)
    up_other = jnp.concatenate([near_first, near_second], axis=1)
    w_up = in_place(up_half, up_other, near).reshape(width, share)
    m_halves, t_sides, w_up, d_inner = meet(m_halves, t_sides, w_up, d_inner)
    t_corners = gather_2(t_sides)
    hidden_m = gather_all(m_pair, m_halves)
    t_corners, hidden_m = meet(t_corners, hidden_m)
    t_halves = gather_3(t_pair, t_sides, t_corners)

    wide = -(-share // 128) * 128
    half = length // 2
    mixed_send = mixed.reshape(block_len, n_ctx, q_cols).transpose(1, 0, 2)
    mixed_send, t_halves = meet(mixed_send, t_halves)
    mixed_cols = exchange(mixed_send, CTX)
    inner_m, d_gu_m, m_keep, m_give = feed_forward(hidden_m, d_inner, 2 * devices, w_gate, w_up, wide)
    m_give, t_halves = meet(m_give, t_halves)
    m_came = send(m_give, "core", 1)
    hidden_t = gather_all(t_pair, t_halves)
    inner_t, d_gu_t, t_keep, t_give = feed_forward(hidden_t, d_inner, 2 * devices + 1, w_gate, w_up, wide)
    t_give, m_keep, m_came, mixed_cols, inner_m = meet(t_give, m_keep, m_came, mixed_cols, inner_m)
    t_came = send(t_give, "core", 1)
    m_back = scatter_1(m_keep, m_came, block_len)
    places = order_ctx(True)
    inner_rows = jnp.concatenate([inner_m, inner_t]).reshape(2 * n_ctx, block_len, wide)
    inner_rows = pick_blocks(inner_rows, jnp.stack([places, places + n_ctx], axis=1).reshape(-1))
    inner_rows, t_keep, t_came, m_back, m_keep, m_came, inner_m, inner_t = meet(
        inner_rows, t_keep, t_came, m_back, m_keep, m_came, inner_m, inner_t
    )
    t_back = scatter_1(t_keep, t_came, block_len)
    m_sides = scatter_2(m_keep, m_came, m_back, block_len)
    out_give = dot(jnp.concatenate([inner_m[half:, :share], inner_t[half:, :share]]), w_dn).astype(BF16)
    out_keep = dot(jnp.concatenate([inner_m[:half, :share], inner_t[:half, :share]]), w_dn).astype(BF16)
    out_give, out_keep, t_back, t_keep, t_came, d_gu_m, d_gu_t = meet(
        out_give, out_keep, t_back, t_keep, t_came, d_gu_m, d_gu_t
    )
    t_sides = scatter_2(t_keep, t_came, t_back, block_len)

    ffn_grad = weight_gradients(
        (hidden_m, hidden_t),
        (d_gu_m, d_gu_t),
        final_rows,
        inner_rows.reshape(2 * length, wide),
        n_far,
        n_near,
    )
    ffn_grad, t_sides, m_sides, t_keep, t_came = meet(ffn_grad, t_sides, m_sides, t_keep, t_came)
    t_other = scatter_3(t_sides)
    m_other = scatter_3(m_sides)
    theirs = scatter_4(t_keep, t_came, t_sides, t_other, block_len).astype(BF16)
    theirs = send(theirs, "far", 1)
    m_other, theirs = meet(m_other, theirs)
    ffn_grad = lax.psum_scatter(ffn_grad, "near", scatter_dimension=0, tiled=True)
    d_hidden2 = scatter_4(m_keep, m_came, m_sides, m_other, block_len) + theirs.astype(F32)

    d_middle = d_final.astype(F32) + norm_backward(d_hidden2, normed2, scale2)
    d_gain2 = jnp.sum(d_hidden2 * normed2, axis=0) / gain2
    d_bias = jnp.sum(d_middle, axis=0)
    d_low = d_middle.astype(BF16)
    d_low, out_give = meet(d_low, out_give)
    l_pair = gather_0(d_low)
    l_pair, d_low, out_give = meet(l_pair, d_low, out_give)
    l_sides = gather_1(l_pair)
    o_came = send(out_give, "core", 1)
    d_mixed = dot_last(d_low, full_out).astype(BF16)
    d_mixed, o_came = meet(d_mixed, o_came)
    o_back = scatter_1(out_keep, o_came, block_len)
    d_mixed = d_mixed.reshape(block_len, NH, HD)
    scores = jnp.einsum("qhd,kd->hqk", query, key, preferred_element_type=F32)
    scores = jnp.where(allowed[None], scores, NEG)
    probs = jnp.exp(scores - log_total)
    probs_again = probs.astype(BF16)
    d_probs = jnp.einsum("qhd,kd->hqk", d_mixed, value, preferred_element_type=F32)
    delta = jnp.sum(probs * d_probs, axis=-1, keepdims=True)
    d_scores = (probs * (d_probs - delta)).astype(BF16)
    d_query = jnp.einsum("hqk,kd->qhd", d_scores, key, preferred_element_type=F32) * q_scale
    d_key = jnp.einsum("hqk,qhd->kd", d_scores, query, preferred_element_type=F32)
    d_value = jnp.einsum("hqk,qhd->kd", probs_again, d_mixed, preferred_element_type=F32)
    d_query = d_query.reshape(block_len, n_ctx, q_cols).astype(BF16).transpose(1, 0, 2)
    d_keyval = jnp.concatenate([d_key, d_value], axis=1).astype(BF16)
    d_keyval = d_keyval.reshape(n_ctx, block_len, n_ctx, kv_cols).transpose(2, 1, 0, 3)
    d_keyval = d_keyval.reshape(n_ctx, block_len, 2 * HD)
    d_send = jnp.concatenate([d_query, d_keyval], axis=2)
    d_send, l_sides, o_back, out_keep, o_came, mixed_cols = meet(
        d_send, l_sides, o_back, out_keep, o_came, mixed_cols
    )
    came = exchange(d_send, CTX)
    l_corners = gather_2(l_sides)
    o_sides = scatter_2(out_keep, o_came, o_back, block_len)
    mixed_cols = pick_blocks(mixed_cols, devices).reshape(length, q_cols)
    came, l_corners, ffn_grad, mixed_cols = meet(came, l_corners, ffn_grad, mixed_cols)
    ffn_grad = exchange(ffn_grad[0], ("far",))
    l_halves = gather_3(l_pair, l_sides, l_corners)
    d_keyval = jnp.sum(came[:, :, q_cols:].astype(F32), axis=0).astype(BF16)
    d_keyval = d_keyval.reshape(block_len, n_ctx, kv_cols).transpose(1, 0, 2)
    d_qkv = jnp.concatenate([came[:, :, :q_cols], d_keyval], axis=2)
    d_back = pick_blocks(d_qkv, devices).reshape(length, q_cols + kv_cols)
    d_qkv = d_qkv.reshape(length, q_cols + kv_cols)
    e_came = send(dot_last(d_back[half:], w_qkv).astype(BF16), "core", 1)
    e_keep = dot_last(d_back[:half], w_qkv).astype(BF16)
    e_keep, e_came, l_halves, o_sides, d_qkv = meet(e_keep, e_came, l_halves, o_sides, d_qkv)
    e_back = scatter_1(e_keep, e_came, block_len)
    o_other = scatter_3(o_sides)
    attn_grad = two_gradients(hidden1, d_qkv, gather_all(l_pair, l_halves), mixed_cols)
    d_gain1 = attn_grad[:, : q_cols + kv_cols].astype(F32) * w_qkv.astype(F32)
    d_gain1 = jnp.sum(d_gain1, axis=1) / gain1
    e_back, o_other, out_keep, o_came = meet(e_back, o_other, out_keep, o_came)
    e_sides = scatter_2(e_keep, e_came, e_back, block_len)
    sums = jnp.stack([d_gain1, d_bias, d_gain2]).reshape(3, n_all, rows).transpose(1, 0, 2)
    e_sides, attn_grad, sums, ffn_grad = meet(e_sides, attn_grad, sums, ffn_grad)
    attn_grad = lax.psum_scatter(attn_grad, SEQ, scatter_dimension=0, tiled=True)
    e_other = scatter_3(e_sides)
    o_total = scatter_4(out_keep, o_came, o_sides, o_other, block_len)
    o_theirs = send(o_total[block_len:].astype(BF16), "far", 1)
    d_normed1 = scatter_4(e_keep, e_came, e_sides, e_other, block_len)
    d_input = d_middle + norm_backward(d_normed1, normed1, scale1)
    output = (middle + o_total[:block_len] + o_theirs.astype(F32)).astype(BF16)
    count = n_ctx // 2
    odd = position % 2
    gate, up = ffn_grad[:, :, :wide], ffn_grad[:, :, wide : 2 * wide]
    pieces = []
    for flip in range(2):
        pairs = [(c, ((c % 2) ^ flip) * count + c // 2) for c in range(n_ctx)]
        pieces.append(lax.ppermute(jnp.where(odd == flip, gate, up), CTX, pairs))
    down_grad = ffn_grad[:, :, 2 * wide : 2 * wide + share].transpose(0, 2, 1)
    down_grad = down_grad.reshape(n_far * share, quarter).astype(F32)
    upper = position >= count
    columns = [jnp.where(upper, pieces[1], pieces[0]), jnp.where(upper, pieces[0], pieces[1])]
    own_gain = lax.dynamic_slice_in_dim(gain2, (far * n_near + near) * quarter, quarter)
    gateup_grad = (
        jnp.concatenate([columns[i][f][:, :share] for i in range(2) for f in range(n_far)], axis=1).astype(F32)
        * own_gain[:, None]
    )
    sums, d_input, down_grad = meet(sums, d_input, down_grad)
    sums = exchange(sums, EVERY)
    sums, attn_grad, output, gateup_grad = meet(sums, attn_grad, output, gateup_grad)
    sums = jnp.sum(sums, axis=0)
    attn_grad = attn_grad.astype(F32)
    own_gain = lax.dynamic_slice_in_dim(gain1, (far * n_near + near) * quarter, quarter)
    qkv_grad = attn_grad[:, : q_cols + kv_cols] * own_gain[:, None]
    out_grad = attn_grad[:, q_cols + kv_cols :].T
    return (
        output.reshape(1, block_len, width),
        d_input.reshape(1, block_len, width),
        sums[0],
        qkv_grad[:, :q_cols],
        qkv_grad[:, q_cols:],
        out_grad,
        sums[1],
        sums[2],
        gateup_grad,
        down_grad,
    )


def solution(mesh):
    n_ctx, n_seq = mesh.shape["ctx"], mesh.shape["seq"]
    side = math.isqrt(n_ctx // 2)
    fine = Mesh(
        mesh.devices.reshape(n_ctx // 2 // side, side, 2, n_seq // 2, 2), EVERY
    )
    whole = P(EVERY)
    return jax.shard_map(
        per_device,
        mesh=fine,
        in_specs=(
            P(SEQ, CTX, None),
            P(SEQ, CTX, None),
            whole,
            whole,
            whole,
            whole,
            whole,
            whole,
            whole,
            whole,
        ),
        out_specs=(
            P(SEQ, CTX, None),
            P(SEQ, CTX, None),
            whole,
            P(SEQ, CTX),
            P(SEQ, CTX),
            P(CTX, SEQ),
            whole,
            whole,
            P(SEQ, CTX),
            P(CTX, SEQ),
        ),
        check_vma=False,
    )
```
